256 devices in a mesh: dp: 4 (over y), seq: 16 (over z, core), mp: 4 (over x).
Axes of the slice: x: 4, y: 4, z: 8, core: 2. Of those that a mesh axis runs over, the one named last changes fastest.
Arguments:
- q_self: bfloat16 [4, 1024, 4096], P('dp', 'seq', 'mp'), may hold values from -12 to 12
- k_self: bfloat16 [4, 1024, 4096], P('dp', 'seq', 'mp'), may hold values from -3 to 3
- v_self: bfloat16 [4, 1024, 4096], P('dp', 'seq', 'mp'), may hold values from -0.75 to 0.75
- out_grad_self: bfloat16 [4, 1024, 4096], P('dp', 'seq', 'mp'), may hold values from -6 to 6
- q_cross: bfloat16 [4, 1024, 4096], P('dp', 'seq', 'mp'), may hold values from -12 to 12
- k_cross: bfloat16 [4, 2048, 4096], P('dp', 'seq', 'mp'), may hold values from -3 to 3
- v_cross: bfloat16 [4, 2048, 4096], P('dp', 'seq', 'mp'), may hold values from -0.75 to 0.75
- out_grad_cross: bfloat16 [4, 1024, 4096], P('dp', 'seq', 'mp'), may hold values from -8 to 8
- dec_lengths: int32 [4, 16], P('dp'), may hold values from 1 to 640, as said below
- enc_lengths: int32 [4, 16], P('dp'), may hold values from 1 to 1280, as said below
- rel_bias: float32 [32, 64], P(None, 'mp'), may hold values from -4 to 4
Outputs:
- grad_q_self: bfloat16 [4, 1024, 4096], P('dp', 'seq', 'mp')
- grad_k_self: bfloat16 [4, 1024, 4096], P('dp', 'seq', 'mp')
- grad_v_self: bfloat16 [4, 1024, 4096], P('dp', 'seq', 'mp')
- grad_q_cross: bfloat16 [4, 1024, 4096], P('dp', 'seq', 'mp')
- grad_k_cross: bfloat16 [4, 2048, 4096], P('dp', 'seq', 'mp')
- grad_v_cross: bfloat16 [4, 2048, 4096], P('dp', 'seq', 'mp')
- bias_grad: float32 [32, 64], P(None, 'mp')
The draws below stay inside these ranges and needn't reach their ends.
Inputs may be any that keep to these rules, and one draw needn't show every extreme that they name: `dec_lengths`: row p lists the decoder lengths of the 16 examples of pack p in order; they sum to 1024 and the largest is exactly 640. `enc_lengths`: row p lists the encoder lengths of the same 16 examples in the same order; they sum to 2048. The example with 640 decoder rows has exactly 1280 encoder rows; every other example has at least as many encoder rows as decoder rows and at most three times as many.
All inputs are finite; a program needn't handle non-finite values.
Results may differ from the reference program's by a relative error of at most 0.039.
Values may be sent and summed in bfloat16 or wider, within the bound.
A program may use at most 128 MiB of HBM per device.

```python
import math
import jax
import jax.numpy as jnp
from jax import lax

HEADS = 64
HEAD_DIM = 64
BUCKETS = 32
DISTANCE = 128
DEC_DEV = 64
NEX = 16
PACKS = 4
DEC = 1024
ENC = 2048
DMOST = 640
EMOST = 1280
FEAT = 4096
N_SEQ = 16


def pack_lengths(key):
    base_key = jax.random.fold_in(key, 7)
    cut_key, top_key, shift_key = jax.random.split(base_key, 3)
    remainder = DEC - DMOST
    others = NEX - 1
    slot_count = remainder - 1
    ceiling = max(2, (1 << 30) // max(slot_count, 1))
    raw_draw = jax.random.randint(cut_key, (PACKS, slot_count), 0, ceiling, dtype=jnp.int32)
    distinct = raw_draw * slot_count + jnp.arange(slot_count, dtype=jnp.int32)[None, :]
    unused_values, chosen = lax.top_k(distinct, others - 1)
    cut_points = chosen.astype(jnp.int32) + 1
    negated, unused_order = lax.top_k(-cut_points, others - 1)
    ascending = -negated
    bounds = jnp.concatenate([jnp.zeros((PACKS, 1), jnp.int32), ascending, jnp.full((PACKS, 1), remainder, jnp.int32)], axis=1)
    other_spans = (bounds[:, 1:] - bounds[:, :-1]).astype(jnp.int32)
    top_index = jax.random.randint(top_key, (PACKS, 1), 0, NEX, dtype=jnp.int32)
    slot_index = jnp.arange(NEX, dtype=jnp.int32)[None, :]
    source = jnp.clip(slot_index - (slot_index > top_index).astype(jnp.int32), 0, others - 1)
    source = jnp.broadcast_to(source, (PACKS, NEX)).astype(jnp.int32)
    dec_rows = jnp.take_along_axis(other_spans, source, axis=1)
    dec_result = jnp.where(slot_index == top_index, DMOST, dec_rows).astype(jnp.int32)
    previous = jnp.roll(other_spans, 1, axis=1)
    shift_cap = jnp.minimum(other_spans, previous)
    shifts = jax.random.randint(shift_key, (PACKS, others), 0, shift_cap + 1, dtype=jnp.int32)
    enc_spans = 2 * other_spans + shifts - jnp.roll(shifts, -1, axis=1)
    enc_rows = jnp.take_along_axis(enc_spans, source, axis=1)
    enc_result = jnp.where(slot_index == top_index, EMOST, enc_rows).astype(jnp.int32)
    return (dec_result, enc_result)


def aligned_pair(key, salt, cross):
    base_key = jax.random.fold_in(key, salt)
    flat_key = jax.random.fold_in(base_key, 0)
    query_key = jax.random.fold_in(base_key, 3)
    noise_key = jax.random.fold_in(base_key, 5)
    feature_count = HEADS * HEAD_DIM
    key_total = ENC if cross else DEC
    flat_pack = jax.random.randint(flat_key, (), 0, PACKS, dtype=jnp.int32)
    flat_mask = jnp.arange(PACKS, dtype=jnp.int32)[:, None, None] == flat_pack
    queries = 0.45 * jax.random.truncated_normal(query_key, -6.0, 6.0, (PACKS, DEC, feature_count), jnp.float32)
    queries = jnp.where(flat_mask, 0.02 * queries, queries)
    key_rows = 0.45 * jax.random.truncated_normal(noise_key, -6.0, 6.0, (PACKS, key_total, feature_count), jnp.float32)
    return (queries, key_rows)


def draw_q_self(key, part):
    return aligned_pair(key, 11, False)[0].astype(jnp.bfloat16)


def draw_k_self(key, part):
    return aligned_pair(key, 11, False)[1].astype(jnp.bfloat16)


def draw_q_cross(key, part):
    return aligned_pair(key, 12, True)[0].astype(jnp.bfloat16)


def draw_k_cross(key, part):
    return aligned_pair(key, 12, True)[1].astype(jnp.bfloat16)


def draw_out_grad_cross(key, part):
    base_key = jax.random.fold_in(key, 13)
    noise_key = jax.random.fold_in(base_key, 1)
    feature_count = HEADS * HEAD_DIM
    grads = jax.random.truncated_normal(noise_key, -6.0, 6.0, (PACKS, DEC, feature_count), jnp.float32)
    return grads.astype(jnp.bfloat16)


def draw_dec_lengths(key, part):
    return pack_lengths(key)[0]


def draw_enc_lengths(key, part):
    return pack_lengths(key)[1]


def levels(own_key, shape, cuts, low, top_value):
    factor_of, own = 1.0, jax.random.fold_in(own_key, 6)
    for dim, blocks in cuts:
        heights = jnp.exp(jax.random.uniform(jax.random.fold_in(own, dim), (blocks,), jnp.float32, low / len(cuts), top_value / len(cuts)))
        factor_of = factor_of * jnp.repeat(heights, shape[dim] // blocks).reshape([-1 if axis == dim else 1 for axis in range(len(shape))])
    return factor_of


def centred(stream_key, dims, spread, most, shards=(), kind=jnp.bfloat16):
    factor_of = levels(stream_key, dims, shards, -0.22, 0.18) if shards else 1.0
    entries = jax.random.normal(stream_key, dims, jnp.float32) * spread * factor_of
    return jnp.minimum(jnp.maximum(entries, -most), most).astype(kind)


def setup_inputs(seed: int = 0) -> dict:
    key_list = jax.random.split(jax.random.key(seed), 12)
    q_self = draw_q_self(jax.random.fold_in(key_list[11], 71), 0)
    k_self = draw_k_self(jax.random.fold_in(key_list[11], 71), 0)
    v_self = centred(key_list[2], (PACKS, DEC, FEAT), 0.125, 0.75, ((0, 4), (1, 16), (2, 4)))
    out_grad_self = centred(key_list[3], (PACKS, DEC, FEAT), 1.0, 6.0, ((0, 4), (1, 16), (2, 4)))
    q_cross = draw_q_cross(jax.random.fold_in(key_list[11], 71), 0)
    k_cross = draw_k_cross(jax.random.fold_in(key_list[11], 71), 0)
    v_cross = centred(key_list[6], (PACKS, ENC, FEAT), 0.125, 0.75, ((0, 4), (1, 16), (2, 4)))
    out_grad_cross = draw_out_grad_cross(jax.random.fold_in(key_list[11], 71), 0)
    dec_lengths = draw_dec_lengths(jax.random.fold_in(key_list[11], 71), 0)
    enc_lengths = draw_enc_lengths(jax.random.fold_in(key_list[11], 71), 0)
    rel_bias = centred(key_list[10], (BUCKETS, HEADS), 1.0, 4.0, ((1, 4),), jnp.float32)
    return dict(q_self=q_self, k_self=k_self, v_self=v_self, out_grad_self=out_grad_self, q_cross=q_cross, k_cross=k_cross, v_cross=v_cross, out_grad_cross=out_grad_cross, dec_lengths=dec_lengths, enc_lengths=enc_lengths, rel_bias=rel_bias)


def bucket_of(distances):
    exact_count = BUCKETS // 2
    bucketed = jnp.full(distances.shape, exact_count, jnp.int32)
    for level_index in range(1, BUCKETS - exact_count):
        threshold = math.ceil(exact_count * (DISTANCE / exact_count) ** (level_index / (BUCKETS - exact_count)))
        bucketed = bucketed + (distances >= threshold).astype(jnp.int32)
    return jnp.where(distances < exact_count, distances, bucketed).astype(jnp.int32)

def example_ids(total_rows, lengths):
    segment_ends = jnp.cumsum(lengths).astype(jnp.int32)
    positions = jnp.arange(total_rows, dtype=jnp.int32)
    return lax.optimization_barrier(jnp.sum((positions[:, None] >= segment_ends[None, :]).astype(jnp.int32), axis=1)).astype(jnp.int32)

def rounded(tensor):
    return lax.optimization_barrier(tensor.astype(jnp.bfloat16)).astype(jnp.float32)

def pack_grads(queries, keys, values, out_grads, query_ids, key_ids, rel_bias, causal):
    highest = lax.Precision.HIGHEST
    key_count = keys.shape[0]
    key_full = keys.reshape(key_count, HEADS, HEAD_DIM).astype(jnp.float32)
    value_full = values.reshape(key_count, HEADS, HEAD_DIM).astype(jnp.float32)
    key_pos = jnp.arange(key_count, dtype=jnp.int32)
    bucket_ids = jnp.arange(BUCKETS, dtype=jnp.int32)

    def shard_step(running, shard_id):
        key_sum, value_sum, bias_sum = running
        first_row = shard_id * DEC_DEV
        query_block = lax.dynamic_slice_in_dim(queries, first_row, DEC_DEV, 0).reshape(DEC_DEV, HEADS, HEAD_DIM).astype(jnp.float32)
        grad_block = lax.dynamic_slice_in_dim(out_grads, first_row, DEC_DEV, 0).reshape(DEC_DEV, HEADS, HEAD_DIM).astype(jnp.float32)
        block_ids = lax.dynamic_slice_in_dim(query_ids, first_row, DEC_DEV, 0)
        query_pos = first_row + jnp.arange(DEC_DEV, dtype=jnp.int32)
        scores = jnp.einsum('thd,uhd->htu', query_block, key_full, precision=highest)
        allowed = block_ids[:, None] == key_ids[None, :]
        one_hot = jnp.zeros((1, 1, 1), jnp.float32)
        if causal:
            distances = query_pos[:, None] - key_pos[None, :]
            allowed = allowed & (distances >= 0)
            buckets = bucket_of(jnp.maximum(distances, 0))
            one_hot = (buckets[None] == bucket_ids[:, None, None]).astype(jnp.float32)
            scores = scores + jnp.einsum('bh,btu->htu', rel_bias, one_hot, precision=highest)
        scores = jnp.where(allowed[None], scores, -jnp.inf)
        row_high = lax.optimization_barrier(jnp.max(scores, axis=2, keepdims=True))
        exponent = jnp.exp(scores - row_high)
        weights = exponent / lax.optimization_barrier(jnp.sum(exponent, axis=2, keepdims=True))
        narrow_weights = rounded(weights)
        outputs = rounded(jnp.einsum('htu,uhd->thd', narrow_weights, value_full, precision=highest))
        row_delta = jnp.einsum('thd,thd->ht', grad_block, outputs, precision=highest)
        weight_grads = jnp.einsum('thd,uhd->htu', grad_block, value_full, precision=highest)
        score_grads = weights * (weight_grads - row_delta[:, :, None])
        narrow_grads = rounded(score_grads)
        query_grad = jnp.einsum('htu,uhd->thd', narrow_grads, key_full, precision=highest).astype(jnp.bfloat16)
        key_sum = key_sum + rounded(jnp.einsum('htu,thd->uhd', narrow_grads, query_block, precision=highest))
        value_sum = value_sum + rounded(jnp.einsum('htu,thd->uhd', narrow_weights, grad_block, precision=highest))
        if causal:
            bias_sum = bias_sum + jnp.einsum('htu,btu->bh', score_grads, one_hot, precision=highest)
        return ((key_sum, value_sum, bias_sum), query_grad)
    start_state = (jnp.zeros((key_count, HEADS, HEAD_DIM), jnp.float32), jnp.zeros((key_count, HEADS, HEAD_DIM), jnp.float32), jnp.zeros((BUCKETS, HEADS), jnp.float32))
    (key_sum, value_sum, bias_sum), query_grads = lax.scan(shard_step, start_state, jnp.arange(N_SEQ, dtype=jnp.int32))
    feature_count = HEADS * HEAD_DIM
    return (query_grads.reshape(DEC, feature_count), key_sum.astype(jnp.bfloat16).reshape(key_count, feature_count), value_sum.astype(jnp.bfloat16).reshape(key_count, feature_count), bias_sum)

def reference(q_self, k_self, v_self, out_grad_self, q_cross, k_cross, v_cross, out_grad_cross, dec_lengths, enc_lengths, rel_bias):
    self_q_list = []
    self_k_list = []
    self_v_list = []
    cross_q_list = []
    cross_k_list = []
    cross_v_list = []
    bias_total = jnp.zeros((BUCKETS, HEADS), jnp.float32)
    for pack_index in range(PACKS):
        dec_ids = example_ids(DEC, dec_lengths[pack_index])
        enc_ids = example_ids(ENC, enc_lengths[pack_index])
        query_grad, key_grad, value_grad, bias_part = pack_grads(q_self[pack_index], k_self[pack_index], v_self[pack_index], out_grad_self[pack_index], dec_ids, dec_ids, rel_bias, True)
        self_q_list.append(query_grad)
        self_k_list.append(key_grad)
        self_v_list.append(value_grad)
        bias_total = bias_total + bias_part
        query_grad, key_grad, value_grad, bias_part = pack_grads(q_cross[pack_index], k_cross[pack_index], v_cross[pack_index], out_grad_cross[pack_index], dec_ids, enc_ids, rel_bias, False)
        cross_q_list.append(query_grad)
        cross_k_list.append(key_grad)
        cross_v_list.append(value_grad)
    bias_grad = bias_total / math.sqrt(PACKS * DEC)
    return (jnp.stack(self_q_list), jnp.stack(self_k_list), jnp.stack(self_v_list), jnp.stack(cross_q_list), jnp.stack(cross_k_list), jnp.stack(cross_v_list), bias_grad)
```

```python
import functools
import math

import jax
import jax.numpy as jnp
from jax import lax
from jax.experimental import pallas as pl
from jax.experimental.pallas import tpu as pltpu
from jax.sharding import PartitionSpec as P

HD = 64
BUCKETS = 32
DISTANCE = 128
NEX = 16
N = 16
DEC = 1024
ENC = 2048
DROW = DEC // N
EROW = ENC // N
BIG = 131072.0
BF = jnp.bfloat16
F32 = jnp.float32
VM = pl.BlockSpec(memory_space=pltpu.VMEM)
SM = pl.BlockSpec(memory_space=pltpu.SMEM)

STEPS = [
    (dz, dc)
    for dz in (3, 5, 4, 2, 6, 1, 7, 0)
    for dc in (0, 1)
    if (dz, dc) != (0, 0)
]


def thresholds():
    half = BUCKETS // 2
    lows = list(range(half + 1))
    for level in range(1, BUCKETS - half):
        lows.append(math.ceil(half * (DISTANCE / half) ** (level / (BUCKETS - half))))
    return lows


LOWS = thresholds()


def swap_halves(x):
    return jnp.concatenate([x[:, HD:], x[:, :HD]], axis=1)


def left_lanes(rows):
    return lax.broadcasted_iota(jnp.int32, (rows, 128), 1) < HD


def dot(a, b):
    return jnp.dot(a, b, preferred_element_type=F32)


def place():
    me = lax.axis_index("seq")
    return me, lax.div(me, 2), lax.rem(me, 2)


def target_of(dz, dc):
    me, z, c = place()
    return lax.rem(z + dz, N // 2) * 2 + lax.rem(c + dc, 2)


def meet(with_dp):
    barrier = pltpu.get_barrier_semaphore()
    for dz, dc in STEPS:
        pl.semaphore_signal(
            barrier,
            inc=1,
            device_id={"seq": target_of(dz, dc)},
            device_id_type=pl.DeviceIdType.MESH,
        )
    if with_dp:
        for k in range(1, 4):
            pl.semaphore_signal(
                barrier,
                inc=1,
                device_id={"dp": lax.rem(lax.axis_index("dp") + k, 4)},
                device_id_type=pl.DeviceIdType.MESH,
            )
    pl.semaphore_wait(barrier, len(STEPS) + (3 if with_dp else 0))


def seq_copy(src, dst, send_sem, recv_sem, which, step):
    dz, dc = step
    return pltpu.make_async_remote_copy(
        src_ref=src,
        dst_ref=dst,
        send_sem=send_sem.at[which, dz * 2 + dc],
        recv_sem=recv_sem.at[which, dz * 2 + dc],
        device_id={"seq": target_of(dz, dc)},
        device_id_type=pl.DeviceIdType.MESH,
    )


def pack_heads(a_ref, b_ref, out_ref):
    rows = a_ref.shape[0]
    left = left_lanes(rows)
    for pair in range(N // 2):
        a = a_ref[:, pair * 128 : pair * 128 + 128]
        b = b_ref[:, pair * 128 : pair * 128 + 128]
        out_ref[2 * pair] = jnp.where(left, a, swap_halves(b))
        out_ref[2 * pair + 1] = jnp.where(left, swap_halves(a), b)


def gather_kernel(
    q_s, k_s, v_s, g_s, q_c, k_c, v_c, g_c, x1, x2, x3, x4, p1, p2, p3, p4, send_sem, recv_sem
):
    me, z, c = place()
    pack_heads(q_s, k_s, p1)
    pack_heads(v_s, g_s, p2)
    pack_heads(q_c, g_c, p3)
    pack_heads(k_c, v_c, p4)
    meet(False)
    copies = []
    for which, (src, dst, rows) in enumerate(
        ((p1, x1, DROW), (p2, x2, DROW), (p3, x3, DROW), (p4, x4, EROW))
    ):
        for step in STEPS:
            copy = seq_copy(
                src.at[target_of(*step)],
                dst.at[pl.ds(me * rows, rows)],
                send_sem,
                recv_sem,
                which,
                step,
            )
            copy.start()
            copies.append(copy)
    for src, dst, rows in ((p1, x1, DROW), (p2, x2, DROW), (p3, x3, DROW), (p4, x4, EROW)):
        dst[pl.ds(me * rows, rows), :] = src[me]
    for copy in copies:
        copy.wait()


def gather_heads(*arrays):
    return pl.pallas_call(
        gather_kernel,
        out_shape=[
            jax.ShapeDtypeStruct((DEC, 128), BF),
            jax.ShapeDtypeStruct((DEC, 128), BF),
            jax.ShapeDtypeStruct((DEC, 128), BF),
            jax.ShapeDtypeStruct((ENC, 128), BF),
        ],
        in_specs=[VM] * 8,
        out_specs=[VM] * 4,
        scratch_shapes=[
            pltpu.VMEM((N, DROW, 128), BF),
            pltpu.VMEM((N, DROW, 128), BF),
            pltpu.VMEM((N, DROW, 128), BF),
            pltpu.VMEM((N, EROW, 128), BF),
            pltpu.SemaphoreType.DMA((4, N)),
            pltpu.SemaphoreType.DMA((4, N)),
        ],
        compiler_params=pltpu.CompilerParams(collective_id=0, has_side_effects=True),
        name="gather_heads",
    )(*arrays)


def scatter_kernel(
    g1, gqs, gqc, g3, bias, r1, rqs, rqc, r3, rb, dp_part, bias_sum, send_sem, recv_sem, dp_sem
):
    me, z, c = place()
    my_dp = lax.axis_index("dp")
    meet(True)
    dp_copies = []
    for k in range(1, 4):
        copy = pltpu.make_async_remote_copy(
            src_ref=bias,
            dst_ref=dp_part.at[my_dp],
            send_sem=dp_sem.at[0, k],
            recv_sem=dp_sem.at[1, k],
            device_id={"dp": lax.rem(my_dp + k, 4)},
            device_id_type=pl.DeviceIdType.MESH,
        )
        copy.start()
        dp_copies.append(copy)
    dp_part[my_dp] = bias[...]
    copies = []
    jobs = ((g1, r1), (gqs, rqs), (g3, r3), (gqc, rqc))
    for which, (src, dst) in enumerate(jobs):
        if which == 2:
            for copy in dp_copies:
                copy.wait()
            total = ((dp_part[0] + dp_part[1]) + dp_part[2]) + dp_part[3]
            bias_sum[...] = total
            rb[me] = total
        for step in STEPS:
            copy = seq_copy(
                src.at[target_of(*step)], dst.at[me], send_sem, recv_sem, which, step
            )
            copy.start()
            copies.append(copy)
    for step in STEPS:
        copy = seq_copy(bias_sum, rb.at[me], send_sem, recv_sem, 4, step)
        copy.start()
        copies.append(copy)
    for src, dst in jobs:
        dst[me] = src[me]
    for copy in copies:
        copy.wait()


def scatter_rows(g1, gqs, gqc, g3, bias):
    return pl.pallas_call(
        scatter_kernel,
        out_shape=[
            jax.ShapeDtypeStruct((N, DROW, 128), BF),
            jax.ShapeDtypeStruct((N, DROW // 2, 128), BF),
            jax.ShapeDtypeStruct((N, DROW // 2, 128), BF),
            jax.ShapeDtypeStruct((N, EROW, 128), BF),
            jax.ShapeDtypeStruct((N, 1, 128), F32),
        ],
        in_specs=[VM] * 5,
        out_specs=[VM] * 5,
        scratch_shapes=[
            pltpu.VMEM((4, 1, 128), F32),
            pltpu.VMEM((1, 128), F32),
            pltpu.SemaphoreType.DMA((5, N)),
            pltpu.SemaphoreType.DMA((5, N)),
            pltpu.SemaphoreType.DMA((2, 4)),
        ],
        compiler_params=pltpu.CompilerParams(collective_id=1, has_side_effects=True),
        name="scatter_rows",
    )(g1, gqs, gqc, g3, bias)


def unpack_kernel(r1, rqs, rqc, r3, rb, dqs, dks, dvs, dqc, dkc, dvc, dbias):
    def pairs(src, key_out, value_out):
        left = left_lanes(src.shape[1])
        for pair in range(N // 2):
            a, b = src[2 * pair], src[2 * pair + 1]
            key_out[:, pair * 128 : pair * 128 + 128] = jnp.where(left, a, swap_halves(b))
            value_out[:, pair * 128 : pair * 128 + 128] = jnp.where(left, swap_halves(a), b)

    def queries(src, out):
        half = src.shape[1]
        left = left_lanes(half)
        for pair in range(N // 2):
            a, b = src[2 * pair], src[2 * pair + 1]
            out[0:half, pair * 128 : pair * 128 + 128] = jnp.where(left, a, swap_halves(b))
            out[half : 2 * half, pair * 128 : pair * 128 + 128] = jnp.where(
                left, swap_halves(a), b
            )

    pairs(r1, dks, dvs)
    pairs(r3, dkc, dvc)
    queries(rqs, dqs)
    queries(rqc, dqc)
    rows = jnp.concatenate([rb[i] for i in range(N)], axis=0)
    turned = jnp.concatenate([rows, jnp.zeros((128 - N, 128), F32)], axis=0).T
    dbias[...] = turned[:BUCKETS, :N] * (1.0 / math.sqrt(4 * DEC))


def unpack(*arrays):
    dec = jax.ShapeDtypeStruct((DROW, N * HD), BF)
    enc = jax.ShapeDtypeStruct((EROW, N * HD), BF)
    return pl.pallas_call(
        unpack_kernel,
        out_shape=[dec, dec, dec, dec, enc, enc, jax.ShapeDtypeStruct((BUCKETS, N), F32)],
        in_specs=[VM] * 5,
        out_specs=[VM] * 7,
        name="unpack",
    )(*arrays)


def ends_of(lengths):
    ends, total = [], jnp.int32(0)
    for e in range(NEX):
        total = total + lengths[0, e]
        ends.append(total)
    return ends


def key_features(ends, out_ref, rows):
    lane = lax.broadcasted_iota(jnp.int32, (1, 128), 1)
    low = jnp.zeros((1, 128), jnp.int32)
    high = jnp.zeros((1, 128), jnp.int32)
    for e in range(NEX):
        if e:
            low = jnp.where(lane == e, ends[e - 1], low)
        high = jnp.where(lane == e, ends[e], high)
    for first in range(0, rows, 256):
        row = lax.broadcasted_iota(jnp.int32, (256, 128), 0) + first
        inside = (row >= low) & (row < high)
        out_ref[first : first + 256, :] = jnp.where(inside, 1.0, 0.0).astype(BF)


def query_features(ends, out_ref):
    col = lax.broadcasted_iota(jnp.int32, (NEX, DEC), 1)
    sub = lax.broadcasted_iota(jnp.int32, (NEX, DEC), 0)
    low = jnp.zeros((NEX, DEC), jnp.int32)
    high = jnp.zeros((NEX, DEC), jnp.int32)
    for e in range(NEX):
        if e:
            low = jnp.where(sub == e, ends[e - 1], low)
        high = jnp.where(sub == e, ends[e], high)
    inside = (col >= low) & (col < high)
    out_ref[0:NEX, :] = jnp.where(inside, 0.0, -BIG).astype(BF)
    out_ref[NEX:128, :] = jnp.zeros((128 - NEX, DEC), BF)


def bias_tiles(rel_bias, head, tile_ref):
    base = lax.broadcasted_iota(jnp.int32, (128, 128), 1) - lax.broadcasted_iota(
        jnp.int32, (128, 128), 0
    )
    last = rel_bias[BUCKETS - 1, head]
    made = []
    for shift in (0, 128):
        distance = base + shift
        tile = jnp.full((128, 128), rel_bias[0, head] - last, F32)
        for b in range(1, BUCKETS):
            tile = jnp.where(distance >= LOWS[b], rel_bias[b, head] - last, tile)
        made.append(jnp.where(distance >= 0, tile, -BIG))
    near, next_one = made
    zero = jnp.zeros((128, 128), F32)
    tile_ref[0:128, 0:128] = zero
    tile_ref[0:128, 128:256] = zero
    tile_ref[128:256, 0:128] = next_one
    tile_ref[128:256, 128:256] = zero
    tile_ref[256:384, 0:128] = near
    tile_ref[256:384, 128:256] = next_one
    tile_ref[384:512, 0:128] = jnp.full((128, 128), -BIG, F32)
    tile_ref[384:512, 128:256] = near


def bucket_sums(near, next_one, far):
    base = lax.broadcasted_iota(jnp.int32, (128, 128), 1) - lax.broadcasted_iota(
        jnp.int32, (128, 128), 0
    )
    lane = lax.broadcasted_iota(jnp.int32, (1, 128), 1)
    out = jnp.zeros((1, 128), F32)
    for b in range(BUCKETS):
        total = jnp.zeros((1, 128), F32)
        for shift, part in ((0, near), (128, next_one)):
            distance = base + shift
            hit = distance >= LOWS[b]
            if b + 1 < BUCKETS:
                hit = hit & (distance < LOWS[b + 1])
            total = total + jnp.sum(jnp.where(hit, part, 0.0), axis=0, keepdims=True)
        if b + 1 == BUCKETS:
            total = total + far
        out = jnp.where(lane == b, jnp.sum(total, axis=1, keepdims=True), out)
    return out


def turn(src_ref, out_ref, rows):
    for first in range(0, rows, 256):
        out_ref[:, first : first + 256] = src_ref[first : first + 256, :].T


def query_out(grad_ref, out_ref):
    left = left_lanes(DROW // 2)
    for first in range(0, DEC, 256):
        part = grad_ref[:, first : first + 256].astype(BF)
        rows = jnp.concatenate([part, part], axis=0).T
        for i in range(256 // DROW):
            a = rows[i * DROW : i * DROW + DROW // 2]
            b = rows[i * DROW + DROW // 2 : (i + 1) * DROW]
            out_ref[first // DROW + i] = jnp.where(left, a, b)


def finish_rows(high_sum, out_t, grad_t):
    inverse = 1.0 / high_sum
    out_t = out_t * inverse
    scaled = (grad_t.astype(F32) * inverse).astype(BF)
    delta = jnp.sum(scaled.astype(F32) * out_t, axis=0, keepdims=True)
    zero = jnp.zeros_like(scaled)
    rows = jnp.concatenate([zero, scaled], axis=0).T
    return scaled, delta, rows


def compute_kernel(
    x1, x2, x3, x4, dec_len, enc_len, rel_bias,
    g1, gqs, gqc, g3, bias_out,
    t1, t2, t3, t4, mk_s, mk_c, mq, tiles, scores, e_s, e_c, sg, delta_ref, rq, rg, dq,
):
    head = lax.axis_index("seq")
    dec_ends = ends_of(dec_len)
    key_features(dec_ends, mk_s, DEC)
    key_features(ends_of(enc_len), mk_c, ENC)
    query_features(dec_ends, mq)
    bias_tiles(rel_bias, head, tiles)
    turn(x1, t1, DEC)
    turn(x2, t2, DEC)
    turn(x3, t3, DEC)
    turn(x4, t4, ENC)
    zeros = jnp.zeros((HD, 256), BF)
    for first in range(0, DEC, 256):
        left = left_lanes(256)
        rq[first : first + 256, :] = jnp.where(left, x1[first : first + 256, :], 0).astype(BF)

    for tb in range(DEC // 256):
        span = slice(tb * 256, tb * 256 + 256)
        right = jnp.concatenate([zeros, t1[0:HD, span], mq[:, span]], axis=0)
        high = jnp.full((1, 256), -4.0 * BIG, F32)
        for cu in range(tb + 1):
            rows = slice(cu * 256, cu * 256 + 256)
            s = dot(jnp.concatenate([x1[rows, :], mk_s[rows, :]], axis=1), right)
            if tb - cu < 2:
                at = 256 * (1 - (tb - cu))
                s = s + tiles[at : at + 256, :]
            scores[rows, :] = s
            high = jnp.maximum(high, jnp.max(s, axis=0, keepdims=True))
        total = jnp.zeros((1, 256), F32)
        out_t = jnp.zeros((HD, 256), F32)
        for cu in range(tb + 1):
            rows = slice(cu * 256, cu * 256 + 256)
            e = jnp.exp(scores[rows, :] - high)
            total = total + jnp.sum(e, axis=0, keepdims=True)
            narrow = e.astype(BF)
            e_s[rows, span] = narrow
            out_t = out_t + dot(t2[0:HD, rows], narrow)
        scaled, delta, rows_g = finish_rows(total, out_t, t2[HD:128, span])
        sg[:, span] = scaled
        delta_ref[:, span] = delta
        rg[span, :] = rows_g

    near = jnp.zeros((128, 128), F32)
    next_one = jnp.zeros((128, 128), F32)
    far = jnp.zeros((1, 128), F32)
    dq[...] = jnp.zeros_like(dq)

    def fold(x):
        x = jnp.sum(x, axis=0, keepdims=True)
        return sum(x[:, i : i + 128] for i in range(0, x.shape[1], 128))

    for cu in range(DEC // 256):
        rows = slice(cu * 256, cu * 256 + 256)
        span = slice(cu * 256, DEC)
        width = DEC - cu * 256
        right = jnp.concatenate([sg[:, span], jnp.zeros((HD, width), BF)], axis=0)
        dp = dot(x2[rows, :], right)
        e = e_s[rows, span]
        ds = e.astype(F32) * (dp - delta_ref[:, span])
        narrow = ds.astype(BF)
        g1_part = dot(narrow, rq[span, :]) + dot(e, rg[span, :])
        for i in range(256 // DROW):
            g1[cu * (256 // DROW) + i] = g1_part[i * DROW : (i + 1) * DROW].astype(BF)
        dq[:, span] += dot(t1[HD:128, rows], narrow)
        near = near + ds[0:128, 0:128] + ds[128:256, 128:256]
        next_one = next_one + ds[0:128, 128:256]
        if width > 256:
            next_one = next_one + ds[128:256, 256:384]
            far = far + fold(ds[0:128, 256:]) + fold(ds[128:256, 384:])
    bias_out[...] = bucket_sums(near, next_one, far)
    query_out(dq, gqs)

    for first in range(0, DEC, 256):
        left = left_lanes(256)
        rq[first : first + 256, :] = jnp.where(left, x3[first : first + 256, :], 0).astype(BF)

    def cross_rows(tb, carry):
        span = pl.ds(pl.multiple_of(tb * 256, 256), 256)
        right = jnp.concatenate([t3[0:HD, span], zeros, mq[:, span]], axis=0)
        high = jnp.full((1, 256), -4.0 * BIG, F32)
        for cu in range(ENC // 256):
            rows = slice(cu * 256, cu * 256 + 256)
            s = dot(jnp.concatenate([x4[rows, :], mk_c[rows, :]], axis=1), right)
            scores[rows, :] = s
            high = jnp.maximum(high, jnp.max(s, axis=0, keepdims=True))
        total = jnp.zeros((1, 256), F32)
        out_t = jnp.zeros((HD, 256), F32)
        for cu in range(ENC // 256):
            rows = slice(cu * 256, cu * 256 + 256)
            e = jnp.exp(scores[rows, :] - high)
            total = total + jnp.sum(e, axis=0, keepdims=True)
            narrow = e.astype(BF)
            e_c[rows, span] = narrow
            out_t = out_t + dot(t4[HD:128, rows], narrow)
        scaled, delta, rows_g = finish_rows(total, out_t, t3[HD:128, span])
        sg[:, span] = scaled
        delta_ref[:, span] = delta
        rg[span, :] = rows_g
        return carry

    lax.fori_loop(0, DEC // 256, cross_rows, 0)
    dq[...] = jnp.zeros_like(dq)

    def cross_keys(cu, carry):
        rows = pl.ds(pl.multiple_of(cu * 256, 256), 256)
        right = jnp.concatenate([jnp.zeros((HD, DEC), BF), sg[...]], axis=0)
        dp = dot(x4[rows, :], right)
        e = e_c[rows, :]
        narrow = (e.astype(F32) * (dp - delta_ref[...])).astype(BF)
        part = dot(narrow, rq[...]) + dot(e, rg[...])
        for i in range(256 // EROW):
            g3[cu * (256 // EROW) + i] = part[i * EROW : (i + 1) * EROW].astype(BF)
        dq[...] += dot(t4[0:HD, rows], narrow)
        return carry

    lax.fori_loop(0, ENC // 256, cross_keys, 0)
    query_out(dq, gqc)


def compute(x1, x2, x3, x4, dec_len, enc_len, rel_bias):
    return pl.pallas_call(
        compute_kernel,
        out_shape=[
            jax.ShapeDtypeStruct((N, DROW, 128), BF),
            jax.ShapeDtypeStruct((N, DROW // 2, 128), BF),
            jax.ShapeDtypeStruct((N, DROW // 2, 128), BF),
            jax.ShapeDtypeStruct((N, EROW, 128), BF),
            jax.ShapeDtypeStruct((1, 128), F32),
        ],
        in_specs=[VM] * 4 + [SM] * 3,
        out_specs=[VM] * 5,
        scratch_shapes=[
            pltpu.VMEM((128, DEC), BF),
            pltpu.VMEM((128, DEC), BF),
            pltpu.VMEM((128, DEC), BF),
            pltpu.VMEM((128, ENC), BF),
            pltpu.VMEM((DEC, 128), BF),
            pltpu.VMEM((ENC, 128), BF),
            pltpu.VMEM((128, DEC), BF),
            pltpu.VMEM((512, 256), F32),
            pltpu.VMEM((ENC, 256), F32),
            pltpu.VMEM((DEC, DEC), BF),
            pltpu.VMEM((ENC, DEC), BF),
            pltpu.VMEM((HD, DEC), BF),
            pltpu.VMEM((1, DEC), F32),
            pltpu.VMEM((DEC, 128), BF),
            pltpu.VMEM((DEC, 128), BF),
            pltpu.VMEM((HD, DEC), F32),
        ],
        name="attention_grads",
    )(x1, x2, x3, x4, dec_len, enc_len, rel_bias)


def on_device(q_s, k_s, v_s, g_s, q_c, k_c, v_c, g_c, dec_len, enc_len, rel_bias):
    flat = [x.reshape(x.shape[1], x.shape[2]) for x in (q_s, k_s, v_s, g_s, q_c, k_c, v_c, g_c)]
    x1, x2, x3, x4 = gather_heads(*flat)
    g1, gqs, gqc, g3, bias = compute(x1, x2, x3, x4, dec_len, enc_len, rel_bias)
    outs = unpack(*scatter_rows(g1, gqs, gqc, g3, bias))
    return tuple(x.reshape((1,) + x.shape) for x in outs[:6]) + (outs[6],)


def solution(mesh):
    rows = P("dp", "seq", "mp")
    return jax.shard_map(
        on_device,
        mesh=mesh,
        in_specs=(rows,) * 8 + (P("dp", None), P("dp", None), P(None, "mp")),
        out_specs=(rows,) * 6 + (P(None, "mp"),),
        check_vma=False,
    )
```

```python
import functools
import math

import jax
import jax.numpy as jnp
from jax import lax
from jax.experimental import pallas as pl
from jax.experimental.pallas import tpu as pltpu
from jax.sharding import PartitionSpec as P

HD = 64
BUCKETS = 32
DISTANCE = 128
NEX = 16
N = 16
DEC = 1024
ENC = 2048
DROW = DEC // N
EROW = ENC // N
BIG = 131072.0
BF = jnp.bfloat16
F32 = jnp.float32
VM = pl.BlockSpec(memory_space=pltpu.VMEM)

STEPS = [
    (dz, dc)
    for dz in (3, 5, 4, 2, 6, 1, 7, 0)
    for dc in (0, 1)
    if (dz, dc) != (0, 0)
]


def thresholds():
    half = BUCKETS // 2
    lows = list(range(half + 1))
    for level in range(1, BUCKETS - half):
        lows.append(math.ceil(half * (DISTANCE / half) ** (level / (BUCKETS - half))))
    return lows


LOWS = thresholds()


def swap_halves(x):
    return jnp.concatenate([x[:, HD:], x[:, :HD]], axis=1)


def left_lanes(rows):
    return lax.broadcasted_iota(jnp.int32, (rows, 128), 1) < HD


def dot(a, b):
    return jnp.dot(a, b, preferred_element_type=F32)


def place():
    me = lax.axis_index("seq")
    return me, lax.div(me, 2), lax.rem(me, 2)


def target_of(dz, dc):
    me, z, c = place()
    return lax.rem(z + dz, N // 2) * 2 + lax.rem(c + dc, 2)


def signal_peers():
    barrier = pltpu.get_barrier_semaphore()
    for dz, dc in STEPS:
        pl.semaphore_signal(
            barrier,
            inc=1,
            device_id={"seq": target_of(dz, dc)},
            device_id_type=pl.DeviceIdType.MESH,
        )
    for k in range(1, 4):
        pl.semaphore_signal(
            barrier,
            inc=1,
            device_id={"dp": lax.rem(lax.axis_index("dp") + k, 4)},
            device_id_type=pl.DeviceIdType.MESH,
        )


def wait_peers():
    pl.semaphore_wait(pltpu.get_barrier_semaphore(), len(STEPS) + 3)


def seq_copy(src, dst, send_sem, recv_sem, which, step):
    dz, dc = step
    return pltpu.make_async_remote_copy(
        src_ref=src,
        dst_ref=dst,
        send_sem=send_sem.at[which, dz * 2 + dc],
        recv_sem=recv_sem.at[which, dz * 2 + dc],
        device_id={"seq": target_of(dz, dc)},
        device_id_type=pl.DeviceIdType.MESH,
    )


def pack_heads(a_ref, b_ref, out_ref):
    rows = a_ref.shape[0]
    left = left_lanes(rows)
    for pair in range(N // 2):
        a = a_ref[:, pair * 128 : pair * 128 + 128]
        b = b_ref[:, pair * 128 : pair * 128 + 128]
        out_ref[2 * pair] = jnp.where(left, a, swap_halves(b))
        out_ref[2 * pair + 1] = jnp.where(left, swap_halves(a), b)


def unpack_kernel(r1, rqs, rqc, r3, rb, dqs, dks, dvs, dqc, dkc, dvc, dbias):
    def pairs(src, key_out, value_out):
        left = left_lanes(src.shape[1])
        for pair in range(N // 2):
            a, b = src[2 * pair], src[2 * pair + 1]
            key_out[:, pair * 128 : pair * 128 + 128] = jnp.where(left, a, swap_halves(b))
            value_out[:, pair * 128 : pair * 128 + 128] = jnp.where(left, swap_halves(a), b)

    def queries(src, out):
        half = src.shape[1]
        left = left_lanes(half)
        for pair in range(N // 2):
            a, b = src[2 * pair], src[2 * pair + 1]
            out[0:half, pair * 128 : pair * 128 + 128] = jnp.where(left, a, swap_halves(b))
            out[half : 2 * half, pair * 128 : pair * 128 + 128] = jnp.where(
                left, swap_halves(a), b
            )

    pairs(r1, dks, dvs)
    pairs(r3, dkc, dvc)
    queries(rqs, dqs)
    queries(rqc, dqc)
    rows = jnp.concatenate([rb[i] for i in range(N)], axis=0)
    dbias[...] = rows[:, :BUCKETS] * (1.0 / math.sqrt(4 * DEC))


def unpack(*arrays):
    dec = jax.ShapeDtypeStruct((DROW, N * HD), BF)
    enc = jax.ShapeDtypeStruct((EROW, N * HD), BF)
    return pl.pallas_call(
        unpack_kernel,
        out_shape=[dec, dec, dec, dec, enc, enc, jax.ShapeDtypeStruct((N, BUCKETS), F32)],
        in_specs=[VM] * 5,
        out_specs=[VM] * 7,
        name="unpack",
    )(*arrays)


def iota(shape, axis):
    return lax.broadcasted_iota(jnp.int32, shape, axis)


def bounds_of(length_ref):
    row = jnp.concatenate(
        [length_ref[...].astype(F32), jnp.zeros((1, 128 - NEX), F32)], axis=1
    )
    spread = jnp.broadcast_to(row, (128, 128))
    sub, lane = iota((128, 128), 0), iota((128, 128), 1)
    turned = spread.T
    low_row = jnp.sum(jnp.where(sub < lane, turned, 0.0), axis=0, keepdims=True)
    high_row = jnp.sum(jnp.where(sub <= lane, turned, 0.0), axis=0, keepdims=True)
    low_col = jnp.sum(jnp.where(lane < sub, spread, 0.0), axis=1, keepdims=True)
    high_col = jnp.sum(jnp.where(lane <= sub, spread, 0.0), axis=1, keepdims=True)
    return low_row, high_row, low_col[:NEX], high_col[:NEX]


def key_features(low, high, out_ref, rows):
    low, high = low.astype(jnp.int32), high.astype(jnp.int32)
    for first in range(0, rows, 256):
        row = iota((256, 128), 0) + first
        inside = (row >= low) & (row < high)
        out_ref[first : first + 256, :] = jnp.where(inside, 1.0, 0.0).astype(BF)


def query_features(low, high, out_ref):
    col = iota((NEX, DEC), 1)
    inside = (col >= low.astype(jnp.int32)) & (col < high.astype(jnp.int32))
    out_ref[0:NEX, :] = jnp.where(inside, 0.0, -BIG).astype(BF)
    out_ref[NEX:128, :] = jnp.zeros((128 - NEX, DEC), BF)


def bias_tiles(rel_bias, head, tile_ref):
    base = lax.broadcasted_iota(jnp.int32, (128, 128), 1) - lax.broadcasted_iota(
        jnp.int32, (128, 128), 0
    )
    row = iota((N, BUCKETS), 0)
    table = jnp.sum(jnp.where(row == head, rel_bias[...], 0.0), axis=0, keepdims=True)
    table = table - table[:, BUCKETS - 1 :]
    made = []
    for shift in (0, 128):
        distance = base + shift
        tile = jnp.broadcast_to(table[:, 0:1], (128, 128))
        for b in range(1, BUCKETS):
            tile = jnp.where(distance >= LOWS[b], table[:, b : b + 1], tile)
        made.append(jnp.where(distance >= 0, tile, -BIG))
    near, next_one = made
    zero = jnp.zeros((128, 128), F32)
    tile_ref[0:128, 0:128] = zero
    tile_ref[0:128, 128:256] = zero
    tile_ref[128:256, 0:128] = next_one
    tile_ref[128:256, 128:256] = zero
    tile_ref[256:384, 0:128] = near
    tile_ref[256:384, 128:256] = next_one
    tile_ref[384:512, 0:128] = jnp.full((128, 128), -BIG, F32)
    tile_ref[384:512, 128:256] = near


def bucket_sums(near, next_one, far):
    base = lax.broadcasted_iota(jnp.int32, (128, 128), 1) - lax.broadcasted_iota(
        jnp.int32, (128, 128), 0
    )
    lane = lax.broadcasted_iota(jnp.int32, (1, 128), 1)
    out = jnp.zeros((1, 128), F32)
    for b in range(BUCKETS):
        total = jnp.zeros((1, 128), F32)
        for shift, part in ((0, near), (128, next_one)):
            distance = base + shift
            hit = distance >= LOWS[b]
            if b + 1 < BUCKETS:
                hit = hit & (distance < LOWS[b + 1])
            total = total + jnp.sum(jnp.where(hit, part, 0.0), axis=0, keepdims=True)
        if b + 1 == BUCKETS:
            total = total + far
        out = jnp.where(lane == b, jnp.sum(total, axis=1, keepdims=True), out)
    return out


def turn(src_ref, out_ref, rows):
    for first in range(0, rows, 256):
        out_ref[:, first : first + 256] = src_ref[first : first + 256, :].T


def query_out(grad_ref, out_ref):
    left = left_lanes(DROW // 2)
    for first in range(0, DEC, 256):
        part = grad_ref[:, first : first + 256].astype(BF)
        rows = jnp.concatenate([part, part], axis=0).T
        for i in range(256 // DROW):
            a = rows[i * DROW : i * DROW + DROW // 2]
            b = rows[i * DROW + DROW // 2 : (i + 1) * DROW]
            out_ref[first // DROW + i] = jnp.where(left, a, b)


def finish_rows(high_sum, out_t, grad_t):
    inverse = 1.0 / high_sum
    out_t = out_t * inverse
    scaled = (grad_t.astype(F32) * inverse).astype(BF)
    delta = jnp.sum(scaled.astype(F32) * out_t, axis=0, keepdims=True)
    zero = jnp.zeros_like(scaled)
    rows = jnp.concatenate([zero, scaled], axis=0).T
    return scaled, delta, rows


def self_part(x1, x2, g1, gqs, bias_out, t1, t2, mk_s, mq, tiles, scores, e_s, sg, delta_ref, rq, rg, dq):
    turn(x1, t1, DEC)
    turn(x2, t2, DEC)
    zeros = jnp.zeros((HD, 256), BF)
    for first in range(0, DEC, 256):
        left = left_lanes(256)
        rq[first : first + 256, :] = jnp.where(left, x1[first : first + 256, :], 0).astype(BF)

    for tb in range(DEC // 256):
        span = slice(tb * 256, tb * 256 + 256)
        right = jnp.concatenate([zeros, t1[0:HD, span], mq[:, span]], axis=0)
        high = jnp.full((1, 256), -4.0 * BIG, F32)
        for cu in range(tb + 1):
            rows = slice(cu * 256, cu * 256 + 256)
            s = dot(jnp.concatenate([x1[rows, :], mk_s[rows, :]], axis=1), right)
            if tb - cu < 2:
                at = 256 * (1 - (tb - cu))
                s = s + tiles[at : at + 256, :]
            scores[rows, :] = s
            high = jnp.maximum(high, jnp.max(s, axis=0, keepdims=True))
        total = jnp.zeros((1, 256), F32)
        out_t = jnp.zeros((HD, 256), F32)
        for cu in range(tb + 1):
            rows = slice(cu * 256, cu * 256 + 256)
            e = jnp.exp(scores[rows, :] - high)
            total = total + jnp.sum(e, axis=0, keepdims=True)
            narrow = e.astype(BF)
            e_s[rows, span] = narrow
            out_t = out_t + dot(t2[0:HD, rows], narrow)
        scaled, delta, rows_g = finish_rows(total, out_t, t2[HD:128, span])
        sg[:, span] = scaled
        delta_ref[:, span] = delta
        rg[span, :] = rows_g

    near = jnp.zeros((128, 128), F32)
    next_one = jnp.zeros((128, 128), F32)
    far = jnp.zeros((1, 128), F32)
    dq[...] = jnp.zeros_like(dq)

    def fold(x):
        x = jnp.sum(x, axis=0, keepdims=True)
        return sum(x[:, i : i + 128] for i in range(0, x.shape[1], 128))

    for cu in range(DEC // 256):
        rows = slice(cu * 256, cu * 256 + 256)
        span = slice(cu * 256, DEC)
        width = DEC - cu * 256
        right = jnp.concatenate([sg[:, span], jnp.zeros((HD, width), BF)], axis=0)
        dp = dot(x2[rows, :], right)
        e = e_s[rows, span]
        ds = e.astype(F32) * (dp - delta_ref[:, span])
        narrow = ds.astype(BF)
        part = dot(narrow, rq[span, :]) + dot(e, rg[span, :])
        for i in range(256 // DROW):
            g1[cu * (256 // DROW) + i] = part[i * DROW : (i + 1) * DROW].astype(BF)
        dq[:, span] += dot(t1[HD:128, rows], narrow)
        near = near + ds[0:128, 0:128] + ds[128:256, 128:256]
        next_one = next_one + ds[0:128, 128:256]
        if width > 256:
            next_one = next_one + ds[128:256, 256:384]
            far = far + fold(ds[0:128, 256:]) + fold(ds[128:256, 384:])
    bias_out[...] = bucket_sums(near, next_one, far)
    query_out(dq, gqs)


def cross_rows(x3, x4, t3, t4, mk_c, mq, scores, e_c, sg, delta_ref, rg):
    def block(tb, carry):
        span = pl.ds(pl.multiple_of(tb * 256, 256), 256)
        right = jnp.concatenate([t3[0:HD, span], jnp.zeros((HD, 256), BF), mq[:, span]], axis=0)
        high = jnp.full((1, 256), -4.0 * BIG, F32)
        for cu in range(ENC // 256):
            rows = slice(cu * 256, cu * 256 + 256)
            s = dot(jnp.concatenate([x4[rows, :], mk_c[rows, :]], axis=1), right)
            scores[rows, :] = s
            high = jnp.maximum(high, jnp.max(s, axis=0, keepdims=True))
        total = jnp.zeros((1, 256), F32)
        out_t = jnp.zeros((HD, 256), F32)
        for cu in range(ENC // 256):
            rows = slice(cu * 256, cu * 256 + 256)
            e = jnp.exp(scores[rows, :] - high)
            total = total + jnp.sum(e, axis=0, keepdims=True)
            narrow = e.astype(BF)
            e_c[rows, span] = narrow
            out_t = out_t + dot(t4[HD:128, rows], narrow)
        scaled, delta, rows_g = finish_rows(total, out_t, t3[HD:128, span])
        sg[:, span] = scaled
        delta_ref[:, span] = delta
        rg[span, :] = rows_g
        return carry

    lax.fori_loop(0, DEC // 256, block, 0)


def cross_keys(cu, x4, t4, g3, e_c, sg, delta_ref, rq, rg, dq):
    rows = pl.ds(pl.multiple_of(cu * 256, 256), 256)
    right = jnp.concatenate([jnp.zeros((HD, DEC), BF), sg[...]], axis=0)
    dp = dot(x4[rows, :], right)
    e = e_c[rows, :]
    narrow = (e.astype(F32) * (dp - delta_ref[...])).astype(BF)
    part = dot(narrow, rq[...]) + dot(e, rg[...])
    for i in range(256 // EROW):
        g3[cu * (256 // EROW) + i] = part[i * EROW : (i + 1) * EROW].astype(BF)
    dq[...] += dot(t4[0:HD, rows], narrow)


def fused_kernel(
    q_s, k_s, v_s, g_s, q_c, k_c, v_c, g_c, dec_len, enc_len, rel_bias,
    r1, rqs, rqc, r3, rb,
    aq, ak, av, ag, bq, bk, bv, bg, dec_v, enc_v, rel_v,
    p1, p2, p3, p4, x1, x2, x3, x4, g1, gqs, gqc, g3, bias, dp_part, bias_sum,
    t1, t2, t3, t4, mk_s, mk_c, mq, tiles, scores, e_s, e_c, sg, delta_ref, rq, rg, dq,
    in_sem, send_sem, recv_sem, dp_sem,
):
    me, z, c = place()
    my_dp = lax.axis_index("dp")
    signal_peers()
    loads = []
    pairs = (
        (k_c, bk), (v_c, bv), (q_c, bq), (g_c, bg), (q_s, aq), (k_s, ak), (v_s, av), (g_s, ag),
        (dec_len, dec_v), (enc_len, enc_v), (rel_bias, rel_v),
    )
    for i, (src, dst) in enumerate(pairs):
        load = pltpu.make_async_copy(src, dst, in_sem.at[i])
        load.start()
        loads.append(load)

    def send_all(which, src, dst, rows):
        copies = []
        for step in STEPS:
            slot = dst.at[me] if rows is None else dst.at[pl.ds(me * rows, rows)]
            copy = seq_copy(src.at[target_of(*step)], slot, send_sem, recv_sem, which, step)
            copy.start()
            copies.append(copy)
        return copies

    loads[0].wait()
    loads[1].wait()
    pack_heads(bk, bv, p4)
    loads[2].wait()
    loads[3].wait()
    pack_heads(bq, bg, p3)
    wait_peers()
    sent = []
    in4 = send_all(0, p4, x4, EROW)
    in3 = send_all(1, p3, x3, DROW)
    for load in loads[4:]:
        load.wait()
    pack_heads(aq, ak, p1)
    pack_heads(av, ag, p2)
    x4[pl.ds(me * EROW, EROW), :] = p4[me]
    x3[pl.ds(me * DROW, DROW), :] = p3[me]
    dec_low, dec_high, dec_low_c, dec_high_c = bounds_of(dec_v)
    enc_low, enc_high, unused_low, unused_high = bounds_of(enc_v)
    key_features(dec_low, dec_high, mk_s, DEC)
    in1 = send_all(2, p1, x1, DROW)
    in2 = send_all(3, p2, x2, DROW)
    key_features(enc_low, enc_high, mk_c, ENC)
    query_features(dec_low_c, dec_high_c, mq)
    bias_tiles(rel_v, me, tiles)
    x1[pl.ds(me * DROW, DROW), :] = p1[me]
    x2[pl.ds(me * DROW, DROW), :] = p2[me]

    for copy in in4:
        copy.wait_recv()
    turn(x4, t4, ENC)
    for copy in in3:
        copy.wait_recv()
    turn(x3, t3, DEC)
    for first in range(0, DEC, 256):
        left = left_lanes(256)
        rq[first : first + 256, :] = jnp.where(left, x3[first : first + 256, :], 0).astype(BF)
    cross_rows(x3, x4, t3, t4, mk_c, mq, scores, e_c, sg, delta_ref, rg)
    dq[...] = jnp.zeros_like(dq)
    out3, ready = [], []

    def send_ready():
        for step in ready:
            copy = seq_copy(
                g3.at[target_of(*step)], r3.at[me], send_sem, recv_sem, 4, step
            )
            copy.start()
            out3.append(copy)

    for dz in (4, 3, 5, 2, 6, 1, 7, 0):
        cross_keys(lax.rem(z + dz, N // 2), x4, t4, g3, e_c, sg, delta_ref, rq, rg, dq)
        send_ready()
        ready = [(dz, dc) for dc in (0, 1) if (dz, dc) != (0, 0)]
    query_out(dq, gqc)
    send_ready()
    r3[me] = g3[me]
    rqc[me] = gqc[me]

    for copy in in1 + in2:
        copy.wait_recv()
    outc = send_all(5, gqc, rqc, None)
    self_part(
        x1, x2, g1, gqs, bias, t1, t2, mk_s, mq, tiles, scores, e_s, sg, delta_ref, rq, rg, dq
    )
    dp_copies = []
    for k in range(1, 4):
        copy = pltpu.make_async_remote_copy(
            src_ref=bias,
            dst_ref=dp_part.at[my_dp],
            send_sem=dp_sem.at[0, k],
            recv_sem=dp_sem.at[1, k],
            device_id={"dp": lax.rem(my_dp + k, 4)},
            device_id_type=pl.DeviceIdType.MESH,
        )
        copy.start()
        dp_copies.append(copy)
    dp_part[my_dp] = bias[...]
    out1 = send_all(6, g1, r1, None)
    outs = send_all(7, gqs, rqs, None)
    r1[me] = g1[me]
    rqs[me] = gqs[me]
    for copy in dp_copies:
        copy.wait()
    total = ((dp_part[0] + dp_part[1]) + dp_part[2]) + dp_part[3]
    bias_sum[...] = total
    rb[me] = total
    outb = []
    for step in STEPS:
        copy = seq_copy(bias_sum, rb.at[me], send_sem, recv_sem, 8, step)
        copy.start()
        outb.append(copy)
    for copy in in4 + in3 + in1 + in2:
        copy.wait_send()
    for copy in out3 + outc + out1 + outs + outb:
        copy.wait()


def fused(*arrays):
    vm = pltpu.VMEM
    return pl.pallas_call(
        fused_kernel,
        out_shape=[
            jax.ShapeDtypeStruct((N, DROW, 128), BF),
            jax.ShapeDtypeStruct((N, DROW // 2, 128), BF),
            jax.ShapeDtypeStruct((N, DROW // 2, 128), BF),
            jax.ShapeDtypeStruct((N, EROW, 128), BF),
            jax.ShapeDtypeStruct((N, 1, 128), F32),
        ],
        in_specs=[pl.BlockSpec(memory_space=pl.ANY)] * 11,
        out_specs=[VM] * 5,
        scratch_shapes=[
            *[vm((DROW, N * HD), BF)] * 5,
            *[vm((EROW, N * HD), BF)] * 2,
            vm((DROW, N * HD), BF),
            vm((1, NEX), jnp.int32),
            vm((1, NEX), jnp.int32),
            vm((N, BUCKETS), F32),
            *[vm((N, DROW, 128), BF)] * 3,
            vm((N, EROW, 128), BF),
            *[vm((DEC, 128), BF)] * 3,
            vm((ENC, 128), BF),
            vm((N, DROW, 128), BF),
            *[vm((N, DROW // 2, 128), BF)] * 2,
            vm((N, EROW, 128), BF),
            vm((1, 128), F32),
            vm((4, 1, 128), F32),
            vm((1, 128), F32),
            *[vm((128, DEC), BF)] * 3,
            vm((128, ENC), BF),
            vm((DEC, 128), BF),
            vm((ENC, 128), BF),
            vm((128, DEC), BF),
            vm((512, 256), F32),
            vm((ENC, 256), F32),
            vm((DEC, DEC), BF),
            vm((ENC, DEC), BF),
            vm((HD, DEC), BF),
            vm((1, DEC), F32),
            vm((DEC, 128), BF),
            vm((DEC, 128), BF),
            vm((HD, DEC), F32),
            pltpu.SemaphoreType.DMA((11,)),
            pltpu.SemaphoreType.DMA((9, N)),
            pltpu.SemaphoreType.DMA((9, N)),
            pltpu.SemaphoreType.DMA((2, 4)),
        ],
        compiler_params=pltpu.CompilerParams(collective_id=0, has_side_effects=True),
        name="attention_grads",
    )(*arrays)


def on_device(q_s, k_s, v_s, g_s, q_c, k_c, v_c, g_c, dec_len, enc_len, rel_bias):
    flat = [x.reshape(x.shape[1], x.shape[2]) for x in (q_s, k_s, v_s, g_s, q_c, k_c, v_c, g_c)]
    outs = unpack(*fused(*flat, dec_len, enc_len, rel_bias.T))
    return tuple(x.reshape((1,) + x.shape) for x in outs[:6]) + (outs[6].T,)


def solution(mesh):
    rows = P("dp", "seq", "mp")
    return jax.shard_map(
        on_device,
        mesh=mesh,
        in_specs=(rows,) * 8 + (P("dp", None), P("dp", None), P(None, "mp")),
        out_specs=(rows,) * 6 + (P(None, "mp"),),
        check_vma=False,
    )
```

```python
import functools
import math

import jax
import jax.numpy as jnp
from jax import lax
from jax.experimental import pallas as pl
from jax.experimental.pallas import tpu as pltpu
from jax.sharding import PartitionSpec as P

HD = 64
BUCKETS = 32
DISTANCE = 128
NEX = 16
N = 16
DEC = 1024
ENC = 2048
DROW = DEC // N
EROW = ENC // N
BIG = 131072.0
BF = jnp.bfloat16
F32 = jnp.float32
VM = pl.BlockSpec(memory_space=pltpu.VMEM)

STEPS = [
    (dz, dc)
    for dz in (3, 5, 4, 2, 6, 1, 7, 0)
    for dc in (0, 1)
    if (dz, dc) != (0, 0)
]


def thresholds():
    half = BUCKETS // 2
    lows = list(range(half + 1))
    for level in range(1, BUCKETS - half):
        lows.append(math.ceil(half * (DISTANCE / half) ** (level / (BUCKETS - half))))
    return lows


LOWS = thresholds()


def swap_halves(x):
    return jnp.concatenate([x[:, HD:], x[:, :HD]], axis=1)


def left_lanes(rows):
    return lax.broadcasted_iota(jnp.int32, (rows, 128), 1) < HD


def dot(a, b):
    return jnp.dot(a, b, preferred_element_type=F32)


def place():
    me = lax.axis_index("seq")
    return me, lax.div(me, 2), lax.rem(me, 2)


def target_of(dz, dc):
    me, z, c = place()
    return lax.rem(z + dz, N // 2) * 2 + lax.rem(c + dc, 2)


def signal_peers():
    barrier = pltpu.get_barrier_semaphore()
    for dz, dc in STEPS:
        pl.semaphore_signal(
            barrier,
            inc=1,
            device_id={"seq": target_of(dz, dc)},
            device_id_type=pl.DeviceIdType.MESH,
        )
    for k in range(1, 4):
        pl.semaphore_signal(
            barrier,
            inc=1,
            device_id={"dp": lax.rem(lax.axis_index("dp") + k, 4)},
            device_id_type=pl.DeviceIdType.MESH,
        )


def wait_peers():
    pl.semaphore_wait(pltpu.get_barrier_semaphore(), len(STEPS) + 3)


def seq_copy(src, dst, send_sem, recv_sem, which, step):
    dz, dc = step
    return pltpu.make_async_remote_copy(
        src_ref=src,
        dst_ref=dst,
        send_sem=send_sem.at[which, dz * 2 + dc],
        recv_sem=recv_sem.at[which, dz * 2 + dc],
        device_id={"seq": target_of(dz, dc)},
        device_id_type=pl.DeviceIdType.MESH,
    )


def pack_heads(a_ref, b_ref, out_ref, first):
    rows = a_ref.shape[0]
    left = left_lanes(rows)
    span = slice(first, first + rows)
    for pair in range(N // 2):
        a = a_ref[:, pair * 128 : pair * 128 + 128]
        b = b_ref[:, pair * 128 : pair * 128 + 128]
        out_ref[2 * pair, span] = jnp.where(left, a, swap_halves(b))
        out_ref[2 * pair + 1, span] = jnp.where(left, swap_halves(a), b)


def unpack_kernel(r3, rs, rb, dqs, dks, dvs, dqc, dkc, dvc, dbias):
    def spread(src, first, rows, left_out, left_row, right_out, right_row):
        left = left_lanes(rows)
        span = slice(first, first + rows)
        for pair in range(N // 2):
            a, b = src[2 * pair, span], src[2 * pair + 1, span]
            lanes = slice(pair * 128, pair * 128 + 128)
            left_out[left_row : left_row + rows, lanes] = jnp.where(left, a, swap_halves(b))
            right_out[right_row : right_row + rows, lanes] = jnp.where(left, swap_halves(a), b)

    half = DROW // 2
    spread(r3, 0, EROW, dkc, 0, dvc, 0)
    spread(rs, 0, DROW, dks, 0, dvs, 0)
    spread(rs, DROW, half, dqs, 0, dqs, half)
    spread(rs, DROW + half, half, dqc, 0, dqc, half)
    rows = jnp.concatenate([rb[i] for i in range(N)], axis=0)
    dbias[...] = rows[:, :BUCKETS] * (1.0 / math.sqrt(4 * DEC))


def unpack(*arrays):
    dec = jax.ShapeDtypeStruct((DROW, N * HD), BF)
    enc = jax.ShapeDtypeStruct((EROW, N * HD), BF)
    return pl.pallas_call(
        unpack_kernel,
        out_shape=[dec, dec, dec, dec, enc, enc, jax.ShapeDtypeStruct((N, BUCKETS), F32)],
        in_specs=[VM] * 3,
        out_specs=[VM] * 7,
        compiler_params=pltpu.CompilerParams(vmem_limit_bytes=16 * 1024 * 1024),
        name="unpack",
    )(*arrays)


def iota(shape, axis):
    return lax.broadcasted_iota(jnp.int32, shape, axis)


def bounds_of(length_ref):
    row = jnp.concatenate(
        [length_ref[...].astype(F32), jnp.zeros((1, 128 - NEX), F32)], axis=1
    )
    spread = jnp.broadcast_to(row, (128, 128))
    sub, lane = iota((128, 128), 0), iota((128, 128), 1)
    turned = spread.T
    low_row = jnp.sum(jnp.where(sub < lane, turned, 0.0), axis=0, keepdims=True)
    high_row = jnp.sum(jnp.where(sub <= lane, turned, 0.0), axis=0, keepdims=True)
    low_col = jnp.sum(jnp.where(lane < sub, spread, 0.0), axis=1, keepdims=True)
    high_col = jnp.sum(jnp.where(lane <= sub, spread, 0.0), axis=1, keepdims=True)
    return low_row, high_row, low_col[:NEX], high_col[:NEX]


def key_features(low, high, out_ref, rows):
    low, high = low.astype(jnp.int32), high.astype(jnp.int32)
    for first in range(0, rows, 256):
        row = iota((256, 128), 0) + first
        inside = (row >= low) & (row < high)
        out_ref[first : first + 256, :] = jnp.where(inside, 1.0, 0.0).astype(BF)


def query_features(low, high, out_ref):
    col = iota((NEX, DEC), 1)
    inside = (col >= low.astype(jnp.int32)) & (col < high.astype(jnp.int32))
    out_ref[0:NEX, :] = jnp.where(inside, 0.0, -BIG).astype(BF)
    out_ref[NEX:128, :] = jnp.zeros((128 - NEX, DEC), BF)


def bias_tiles(rel_bias, head, tile_ref):
    base = lax.broadcasted_iota(jnp.int32, (128, 128), 1) - lax.broadcasted_iota(
        jnp.int32, (128, 128), 0
    )
    row = iota((N, BUCKETS), 0)
    table = jnp.sum(jnp.where(row == head, rel_bias[...], 0.0), axis=0, keepdims=True)
    table = table - table[:, BUCKETS - 1 :]
    made = []
    for shift in (0, 128):
        distance = base + shift
        tile = jnp.broadcast_to(table[:, 0:1], (128, 128))
        for b in range(1, BUCKETS):
            tile = jnp.where(distance >= LOWS[b], table[:, b : b + 1], tile)
        made.append(jnp.where(distance >= 0, tile, -BIG))
    near, next_one = made
    zero = jnp.zeros((128, 128), F32)
    tile_ref[0:128, 0:128] = zero
    tile_ref[0:128, 128:256] = zero
    tile_ref[128:256, 0:128] = next_one
    tile_ref[128:256, 128:256] = zero
    tile_ref[256:384, 0:128] = near
    tile_ref[256:384, 128:256] = next_one
    tile_ref[384:512, 0:128] = jnp.full((128, 128), -BIG, F32)
    tile_ref[384:512, 128:256] = near


def bucket_sums(near, next_one, far):
    base = lax.broadcasted_iota(jnp.int32, (128, 128), 1) - lax.broadcasted_iota(
        jnp.int32, (128, 128), 0
    )
    lane = lax.broadcasted_iota(jnp.int32, (1, 128), 1)
    out = jnp.zeros((1, 128), F32)
    for b in range(BUCKETS):
        total = jnp.zeros((1, 128), F32)
        for shift, part in ((0, near), (128, next_one)):
            distance = base + shift
            hit = distance >= LOWS[b]
            if b + 1 < BUCKETS:
                hit = hit & (distance < LOWS[b + 1])
            total = total + jnp.sum(jnp.where(hit, part, 0.0), axis=0, keepdims=True)
        if b + 1 == BUCKETS:
            total = total + far
        out = jnp.where(lane == b, jnp.sum(total, axis=1, keepdims=True), out)
    return out


class Rows:
    def __init__(self, ref, first, count):
        self.ref, self.first, self.count = ref, first, count

    def part(self, index):
        devices = 256 // self.count
        block = self.ref[
            pl.ds(index * devices, devices), self.first : self.first + self.count, :
        ]
        return block.reshape(256, 128)


def turn(rows, out_ref):
    for i in range(N * rows.count // 256):
        out_ref[:, i * 256 : i * 256 + 256] = rows.part(i).T


def left_half(rows, out_ref):
    left = left_lanes(256)
    for i in range(N * rows.count // 256):
        out_ref[i * 256 : i * 256 + 256, :] = jnp.where(left, rows.part(i), 0).astype(BF)


def query_out(grad_ref, out_ref, row):
    left = left_lanes(DROW // 2)
    for first in range(0, DEC, 256):
        part = grad_ref[:, first : first + 256].astype(BF)
        rows = jnp.concatenate([part, part], axis=0).T
        for i in range(256 // DROW):
            a = rows[i * DROW : i * DROW + DROW // 2]
            b = rows[i * DROW + DROW // 2 : (i + 1) * DROW]
            out_ref[first // DROW + i, row : row + DROW // 2] = jnp.where(left, a, b)


def finish_rows(high_sum, out_t, grad_t):
    inverse = 1.0 / high_sum
    out_t = out_t * inverse
    scaled = (grad_t.astype(F32) * inverse).astype(BF)
    delta = jnp.sum(scaled.astype(F32) * out_t, axis=0, keepdims=True)
    zero = jnp.zeros_like(scaled)
    rows = jnp.concatenate([zero, scaled], axis=0).T
    return scaled, delta, rows


def self_part(x1, x2, gs, bias_out, t1, t2, mk_s, mq, tiles, scores, e_s, sg, delta_ref, rq, rg, dq):
    turn(x1, t1)
    turn(x2, t2)
    zeros = jnp.zeros((HD, 256), BF)
    left_half(x1, rq)

    for tb in range(DEC // 256):
        span = slice(tb * 256, tb * 256 + 256)
        right = jnp.concatenate([zeros, t1[0:HD, span], mq[:, span]], axis=0)
        high = jnp.full((1, 256), -4.0 * BIG, F32)
        for cu in range(tb + 1):
            rows = slice(cu * 256, cu * 256 + 256)
            s = dot(jnp.concatenate([x1.part(cu), mk_s[rows, :]], axis=1), right)
            if tb - cu < 2:
                at = 256 * (1 - (tb - cu))
                s = s + tiles[at : at + 256, :]
            scores[rows, :] = s
            high = jnp.maximum(high, jnp.max(s, axis=0, keepdims=True))
        total = jnp.zeros((1, 256), F32)
        out_t = jnp.zeros((HD, 256), F32)
        for cu in range(tb + 1):
            rows = slice(cu * 256, cu * 256 + 256)
            e = jnp.exp(scores[rows, :] - high)
            total = total + jnp.sum(e, axis=0, keepdims=True)
            narrow = e.astype(BF)
            e_s[rows, span] = narrow
            out_t = out_t + dot(t2[0:HD, rows], narrow)
        scaled, delta, rows_g = finish_rows(total, out_t, t2[HD:128, span])
        sg[:, span] = scaled
        delta_ref[:, span] = delta
        rg[span, :] = rows_g

    near = jnp.zeros((128, 128), F32)
    next_one = jnp.zeros((128, 128), F32)
    far = jnp.zeros((1, 128), F32)
    dq[...] = jnp.zeros_like(dq)

    def fold(x):
        x = jnp.sum(x, axis=0, keepdims=True)
        return sum(x[:, i : i + 128] for i in range(0, x.shape[1], 128))

    for cu in range(DEC // 256):
        rows = slice(cu * 256, cu * 256 + 256)
        span = slice(cu * 256, DEC)
        width = DEC - cu * 256
        right = jnp.concatenate([sg[:, span], jnp.zeros((HD, width), BF)], axis=0)
        dp = dot(x2.part(cu), right)
        e = e_s[rows, span]
        ds = e.astype(F32) * (dp - delta_ref[:, span])
        narrow = ds.astype(BF)
        part = dot(narrow, rq[span, :]) + dot(e, rg[span, :])
        for i in range(256 // DROW):
            gs[cu * (256 // DROW) + i, 0:DROW] = part[i * DROW : (i + 1) * DROW].astype(BF)
        dq[:, span] += dot(t1[HD:128, rows], narrow)
        near = near + ds[0:128, 0:128] + ds[128:256, 128:256]
        next_one = next_one + ds[0:128, 128:256]
        if width > 256:
            next_one = next_one + ds[128:256, 256:384]
            far = far + fold(ds[0:128, 256:]) + fold(ds[128:256, 384:])
    bias_out[...] = bucket_sums(near, next_one, far)
    query_out(dq, gs, DROW)


def cross_rows(x4, t3, t4, mk_c, mq, scores, e_c, sg, delta_ref, rg):
    def block(tb, carry):
        span = pl.ds(pl.multiple_of(tb * 256, 256), 256)
        right = jnp.concatenate([t3[0:HD, span], jnp.zeros((HD, 256), BF), mq[:, span]], axis=0)
        high = jnp.full((1, 256), -4.0 * BIG, F32)
        for cu in range(ENC // 256):
            rows = slice(cu * 256, cu * 256 + 256)
            s = dot(jnp.concatenate([x4.part(cu), mk_c[rows, :]], axis=1), right)
            scores[rows, :] = s
            high = jnp.maximum(high, jnp.max(s, axis=0, keepdims=True))
        total = jnp.zeros((1, 256), F32)
        out_t = jnp.zeros((HD, 256), F32)
        for cu in range(ENC // 256):
            rows = slice(cu * 256, cu * 256 + 256)
            e = jnp.exp(scores[rows, :] - high)
            total = total + jnp.sum(e, axis=0, keepdims=True)
            narrow = e.astype(BF)
            e_c[rows, span] = narrow
            out_t = out_t + dot(t4[HD:128, rows], narrow)
        scaled, delta, rows_g = finish_rows(total, out_t, t3[HD:128, span])
        sg[:, span] = scaled
        delta_ref[:, span] = delta
        rg[span, :] = rows_g
        return carry

    lax.fori_loop(0, DEC // 256, block, 0)


def cross_keys(cu, x4, t4, g3, e_c, sg, delta_ref, rq, rg, dq):
    rows = pl.ds(pl.multiple_of(cu * 256, 256), 256)
    right = jnp.concatenate([jnp.zeros((HD, DEC), BF), sg[...]], axis=0)
    dp = dot(x4.part(cu), right)
    e = e_c[rows, :]
    narrow = (e.astype(F32) * (dp - delta_ref[...])).astype(BF)
    part = dot(narrow, rq[...]) + dot(e, rg[...])
    for i in range(256 // EROW):
        g3[cu * (256 // EROW) + i] = part[i * EROW : (i + 1) * EROW].astype(BF)
    dq[...] += dot(t4[0:HD, rows], narrow)


def fused_kernel(
    q_s, k_s, v_s, g_s, q_c, k_c, v_c, g_c, dec_len, enc_len, rel_bias,
    r3, rs, rb,
    aq, ak, av, ag, bq, bk, bv, bg, dec_v, enc_v, rel_v,
    pc, ps, xc, xs, g3, gs, bias, dp_part, bias_sum,
    t1, t2, t3, t4, mk_s, mk_c, mq, tiles, scores, e_s, e_c, sg, delta_ref, rq, rg, dq,
    in_sem, send_sem, recv_sem, dp_sem,
):
    me, z, c = place()
    my_dp = lax.axis_index("dp")
    signal_peers()
    loads = []
    pairs = (
        (k_c, bk), (v_c, bv), (q_c, bq), (g_c, bg), (q_s, aq), (k_s, ak), (v_s, av), (g_s, ag),
        (dec_len, dec_v), (enc_len, enc_v), (rel_bias, rel_v),
    )
    for i, (src, dst) in enumerate(pairs):
        load = pltpu.make_async_copy(src, dst, in_sem.at[i])
        load.start()
        loads.append(load)

    def send_all(which, src, dst, steps):
        copies = []
        for step in steps:
            copy = seq_copy(
                src.at[target_of(*step)], dst.at[me], send_sem, recv_sem, which, step
            )
            copy.start()
            copies.append(copy)
        return copies

    for load in loads[:4]:
        load.wait()
    pack_heads(bk, bv, pc, 0)
    pack_heads(bq, bg, pc, EROW)
    wait_peers()
    in_c = send_all(0, pc, xc, STEPS)
    for load in loads[4:]:
        load.wait()
    pack_heads(aq, ak, ps, 0)
    pack_heads(av, ag, ps, DROW)
    xc[me] = pc[me]
    xs[me] = ps[me]
    dec_low, dec_high, dec_low_c, dec_high_c = bounds_of(dec_v)
    enc_low, enc_high, unused_low, unused_high = bounds_of(enc_v)
    key_features(dec_low, dec_high, mk_s, DEC)
    in_s = send_all(1, ps, xs, STEPS)
    key_features(enc_low, enc_high, mk_c, ENC)
    query_features(dec_low_c, dec_high_c, mq)
    bias_tiles(rel_v, me, tiles)
    x1, x2 = Rows(xs, 0, DROW), Rows(xs, DROW, DROW)
    x3, x4 = Rows(xc, EROW, DROW), Rows(xc, 0, EROW)

    for copy in in_c:
        copy.wait_recv()
    turn(x4, t4)
    turn(x3, t3)
    left_half(x3, rq)
    cross_rows(x4, t3, t4, mk_c, mq, scores, e_c, sg, delta_ref, rg)
    dq[...] = jnp.zeros_like(dq)
    out3, ready = [], []

    for dz in (4, 3, 5, 2, 6, 1, 7, 0):
        cross_keys(lax.rem(z + dz, N // 2), x4, t4, g3, e_c, sg, delta_ref, rq, rg, dq)
        out3 += send_all(2, g3, r3, ready)
        ready = [(dz, dc) for dc in (0, 1) if (dz, dc) != (0, 0)]
    query_out(dq, gs, DROW + DROW // 2)
    out3 += send_all(2, g3, r3, ready)
    r3[me] = g3[me]

    for copy in in_s:
        copy.wait_recv()
    self_part(x1, x2, gs, bias, t1, t2, mk_s, mq, tiles, scores, e_s, sg, delta_ref, rq, rg, dq)
    dp_copies = []
    for k in range(1, 4):
        copy = pltpu.make_async_remote_copy(
            src_ref=bias,
            dst_ref=dp_part.at[my_dp],
            send_sem=dp_sem.at[0, k],
            recv_sem=dp_sem.at[1, k],
            device_id={"dp": lax.rem(my_dp + k, 4)},
            device_id_type=pl.DeviceIdType.MESH,
        )
        copy.start()
        dp_copies.append(copy)
    dp_part[my_dp] = bias[...]
    near = [step for step in STEPS if step[0] in (0, 1, 7)]
    out_s = send_all(3, gs, rs, [step for step in STEPS if step not in near])
    rs[me] = gs[me]
    for copy in dp_copies:
        copy.wait()
    total = ((dp_part[0] + dp_part[1]) + dp_part[2]) + dp_part[3]
    bias_sum[...] = total
    rb[me] = total
    out_s += send_all(3, gs, rs, near[:2])
    for step in STEPS:
        copy = seq_copy(bias_sum, rb.at[me], send_sem, recv_sem, 4, step)
        copy.start()
        out_s.append(copy)
    out_s += send_all(3, gs, rs, near[2:])
    for copy in in_c + in_s:
        copy.wait_send()
    for copy in out3 + out_s:
        copy.wait()


def fused(*arrays):
    vm = pltpu.VMEM
    return pl.pallas_call(
        fused_kernel,
        out_shape=[
            jax.ShapeDtypeStruct((N, EROW, 128), BF),
            jax.ShapeDtypeStruct((N, EROW, 128), BF),
            jax.ShapeDtypeStruct((N, 1, 128), F32),
        ],
        in_specs=[pl.BlockSpec(memory_space=pltpu.HBM)] * 11,
        out_specs=[VM] * 3,
        scratch_shapes=[
            *[vm((DROW, N * HD), BF)] * 5,
            *[vm((EROW, N * HD), BF)] * 2,
            vm((DROW, N * HD), BF),
            vm((1, NEX), jnp.int32),
            vm((1, NEX), jnp.int32),
            vm((N, BUCKETS), F32),
            vm((N, EROW + DROW, 128), BF),
            vm((N, 2 * DROW, 128), BF),
            vm((N, EROW + DROW, 128), BF),
            vm((N, 2 * DROW, 128), BF),
            vm((N, EROW, 128), BF),
            vm((N, 2 * DROW, 128), BF),
            vm((1, 128), F32),
            vm((4, 1, 128), F32),
            vm((1, 128), F32),
            *[vm((128, DEC), BF)] * 3,
            vm((128, ENC), BF),
            vm((DEC, 128), BF),
            vm((ENC, 128), BF),
            vm((128, DEC), BF),
            vm((512, 256), F32),
            vm((ENC, 256), F32),
            vm((DEC, DEC), BF),
            vm((ENC, DEC), BF),
            vm((HD, DEC), BF),
            vm((1, DEC), F32),
            vm((DEC, 128), BF),
            vm((DEC, 128), BF),
            vm((HD, DEC), F32),
            pltpu.SemaphoreType.DMA((11,)),
            pltpu.SemaphoreType.DMA((5, N)),
            pltpu.SemaphoreType.DMA((5, N)),
            pltpu.SemaphoreType.DMA((2, 4)),
        ],
        compiler_params=pltpu.CompilerParams(collective_id=0, has_side_effects=True, vmem_limit_bytes=32 * 1024 * 1024
        ),
        name="attention_grads",
    )(*arrays)


def on_device(q_s, k_s, v_s, g_s, q_c, k_c, v_c, g_c, dec_len, enc_len, rel_bias):
    flat = [x.reshape(x.shape[1], x.shape[2]) for x in (q_s, k_s, v_s, g_s, q_c, k_c, v_c, g_c)]
    operands = [
        pltpu.with_memory_space_constraint(x, pltpu.HBM)
        for x in (*flat, dec_len, enc_len, rel_bias.T)
    ]
    outs = unpack(*fused(*operands))
    return tuple(x.reshape((1,) + x.shape) for x in outs[:6]) + (outs[6].T,)


def solution(mesh):
    rows = P("dp", "seq", "mp")
    return jax.shard_map(
        on_device,
        mesh=mesh,
        in_specs=(rows,) * 8 + (P("dp", None), P("dp", None), P(None, "mp")),
        out_specs=(rows,) * 6 + (P(None, "mp"),),
        check_vma=False,
    )
```

```python
import functools
import math

import jax
import jax.numpy as jnp
from jax import lax
from jax.experimental import pallas as pl
from jax.experimental.pallas import tpu as pltpu
from jax.sharding import PartitionSpec as P

HD = 64
BUCKETS = 32
DISTANCE = 128
NEX = 16
N = 16
DEC = 1024
ENC = 2048
DROW = DEC // N
EROW = ENC // N
BIG = 131072.0
BF = jnp.bfloat16
F32 = jnp.float32
VM = pl.BlockSpec(memory_space=pltpu.VMEM)

STEPS = [
    (dz, dc)
    for dz in (3, 5, 4, 2, 6, 1, 7, 0)
    for dc in (0, 1)
    if (dz, dc) != (0, 0)
]


def thresholds():
    half = BUCKETS // 2
    lows = list(range(half + 1))
    for level in range(1, BUCKETS - half):
        lows.append(math.ceil(half * (DISTANCE / half) ** (level / (BUCKETS - half))))
    return lows


LOWS = thresholds()


def swap_halves(x):
    return jnp.concatenate([x[:, HD:], x[:, :HD]], axis=1)


def left_lanes(rows):
    return lax.broadcasted_iota(jnp.int32, (rows, 128), 1) < HD


def dot(a, b):
    return jnp.dot(a, b, preferred_element_type=F32)


def place():
    me = lax.axis_index("seq")
    return me, lax.div(me, 2), lax.rem(me, 2)


def target_of(dz, dc):
    me, z, c = place()
    return lax.rem(z + dz, N // 2) * 2 + lax.rem(c + dc, 2)


def tell(semaphore, device):
    pl.semaphore_signal(
        semaphore, inc=1, device_id=device, device_id_type=pl.DeviceIdType.MESH
    )


def dp_peer(shift):
    return {"dp": lax.rem(lax.axis_index("dp") + shift, 4)}


NEAR = [step for step in STEPS if step[0] in (0, 1, N // 2 - 1)]


def at_hops(hops):
    return [step for step in STEPS if step[0] in (hops, N // 2 - hops)]


IN_ORDER = NEAR + at_hops(2) + at_hops(3) + at_hops(4)


def greet_near():
    barrier = pltpu.get_barrier_semaphore()
    for step in NEAR:
        tell(barrier, {"seq": target_of(*step)})
    tell(barrier, dp_peer(1))
    tell(barrier, dp_peer(3))


def wait_near():
    pl.semaphore_wait(pltpu.get_barrier_semaphore(), len(NEAR) + 2)


def pass_on(up_sem, down_sem, hops):
    tell(up_sem.at[hops], {"seq": target_of(1, 0)})
    tell(down_sem.at[hops], {"seq": target_of(N // 2 - 1, 0)})


def heard(up_sem, down_sem, hops):
    pl.semaphore_wait(up_sem.at[hops], 1)
    pl.semaphore_wait(down_sem.at[hops], 1)


def seq_copy(src, dst, send_sem, recv_sem, which, step):
    dz, dc = step
    return pltpu.make_async_remote_copy(
        src_ref=src,
        dst_ref=dst,
        send_sem=send_sem.at[which, dz * 2 + dc],
        recv_sem=recv_sem.at[which, dz * 2 + dc],
        device_id={"seq": target_of(dz, dc)},
        device_id_type=pl.DeviceIdType.MESH,
    )


def pack_heads(a_ref, b_ref, out_ref, first):
    rows = a_ref.shape[0]
    left = left_lanes(rows)
    span = slice(first, first + rows)
    for pair in range(N // 2):
        a = a_ref[:, pair * 128 : pair * 128 + 128]
        b = b_ref[:, pair * 128 : pair * 128 + 128]
        out_ref[2 * pair, span] = jnp.where(left, a, swap_halves(b))
        out_ref[2 * pair + 1, span] = jnp.where(left, swap_halves(a), b)


def unpack_kernel(
    r3, rs, rb, dqs, dks, dvs, dqc, dkc, dvc, dbias,
    aqs, aks, avs, aqc, akc, avc, abias, sems,
):
    def spread(src, first, rows, left_out, left_row, right_out, right_row):
        left = left_lanes(rows)
        span = slice(first, first + rows)
        for pair in range(N // 2):
            a, b = src[2 * pair, span], src[2 * pair + 1, span]
            lanes = slice(pair * 128, pair * 128 + 128)
            left_out[left_row : left_row + rows, lanes] = jnp.where(left, a, swap_halves(b))
            right_out[right_row : right_row + rows, lanes] = jnp.where(left, swap_halves(a), b)

    def leave(*which):
        for i in which:
            pltpu.make_async_copy(made[i], outs[i], sems.at[i]).start()

    half = DROW // 2
    outs = (dqs, dks, dvs, dqc, dkc, dvc, dbias)
    made = (aqs, aks, avs, aqc, akc, avc, abias)
    spread(r3, 0, EROW, akc, 0, avc, 0)
    leave(4, 5)
    spread(rs, 0, DROW, aks, 0, avs, 0)
    leave(1, 2)
    rows = jnp.concatenate([rb[i] for i in range(N)], axis=0)
    abias[...] = rows[:, :BUCKETS] * (1.0 / math.sqrt(4 * DEC))
    leave(6)
    spread(rs, DROW, half, aqs, 0, aqs, half)
    spread(rs, DROW + half, half, aqc, 0, aqc, half)
    leave(0, 3)
    for i in range(7):
        pltpu.make_async_copy(made[i], outs[i], sems.at[i]).wait()


def unpack(*arrays):
    shapes = [(DROW, N * HD)] * 4 + [(EROW, N * HD)] * 2 + [(N, BUCKETS)]
    kinds = [BF] * 6 + [F32]
    return pl.pallas_call(
        unpack_kernel,
        out_shape=[jax.ShapeDtypeStruct(x, t) for x, t in zip(shapes, kinds)],
        in_specs=[VM] * 3,
        out_specs=[pl.BlockSpec(memory_space=pl.ANY)] * 7,
        scratch_shapes=[pltpu.VMEM(x, t) for x, t in zip(shapes, kinds)]
        + [pltpu.SemaphoreType.DMA((7,))],
        compiler_params=pltpu.CompilerParams(vmem_limit_bytes=16 * 1024 * 1024),
        name="unpack",
    )(*arrays)


def iota(shape, axis):
    return lax.broadcasted_iota(jnp.int32, shape, axis)


def bounds_of(length_ref):
    row = jnp.concatenate(
        [length_ref[...].astype(F32), jnp.zeros((1, 128 - NEX), F32)], axis=1
    )
    spread = jnp.broadcast_to(row, (128, 128))
    sub, lane = iota((128, 128), 0), iota((128, 128), 1)
    turned = spread.T
    low_row = jnp.sum(jnp.where(sub < lane, turned, 0.0), axis=0, keepdims=True)
    high_row = jnp.sum(jnp.where(sub <= lane, turned, 0.0), axis=0, keepdims=True)
    low_col = jnp.sum(jnp.where(lane < sub, spread, 0.0), axis=1, keepdims=True)
    high_col = jnp.sum(jnp.where(lane <= sub, spread, 0.0), axis=1, keepdims=True)
    return low_row, high_row, low_col[:NEX], high_col[:NEX]


def key_features(low, high, out_ref, rows):
    low, high = low.astype(jnp.int32), high.astype(jnp.int32)
    for first in range(0, rows, 256):
        row = iota((256, 128), 0) + first
        inside = (row >= low) & (row < high)
        out_ref[first : first + 256, :] = jnp.where(inside, 1.0, 0.0).astype(BF)


def query_features(low, high, out_ref):
    col = iota((NEX, DEC), 1)
    inside = (col >= low.astype(jnp.int32)) & (col < high.astype(jnp.int32))
    out_ref[0:NEX, :] = jnp.where(inside, 0.0, -BIG).astype(BF)
    out_ref[NEX:128, :] = jnp.zeros((128 - NEX, DEC), BF)


def bias_tiles(rel_bias, head, tile_ref):
    base = lax.broadcasted_iota(jnp.int32, (128, 128), 1) - lax.broadcasted_iota(
        jnp.int32, (128, 128), 0
    )
    row = iota((N, BUCKETS), 0)
    table = jnp.sum(jnp.where(row == head, rel_bias[...], 0.0), axis=0, keepdims=True)
    table = table - table[:, BUCKETS - 1 :]
    made = []
    for shift in (0, 128):
        distance = base + shift
        tile = jnp.broadcast_to(table[:, 0:1], (128, 128))
        for b in range(1, BUCKETS):
            tile = jnp.where(distance >= LOWS[b], table[:, b : b + 1], tile)
        made.append(jnp.where(distance >= 0, tile, -BIG))
    near, next_one = made
    zero = jnp.zeros((128, 128), F32)
    tile_ref[0:128, 0:128] = zero
    tile_ref[0:128, 128:256] = zero
    tile_ref[128:256, 0:128] = next_one
    tile_ref[128:256, 128:256] = zero
    tile_ref[256:384, 0:128] = near
    tile_ref[256:384, 128:256] = next_one
    tile_ref[384:512, 0:128] = jnp.full((128, 128), -BIG, F32)
    tile_ref[384:512, 128:256] = near


def bucket_sums(near, next_one, far):
    base = lax.broadcasted_iota(jnp.int32, (128, 128), 1) - lax.broadcasted_iota(
        jnp.int32, (128, 128), 0
    )
    lane = lax.broadcasted_iota(jnp.int32, (1, 128), 1)
    out = jnp.zeros((1, 128), F32)
    for b in range(BUCKETS):
        total = jnp.zeros((1, 128), F32)
        for shift, part in ((0, near), (128, next_one)):
            distance = base + shift
            hit = distance >= LOWS[b]
            if b + 1 < BUCKETS:
                hit = hit & (distance < LOWS[b + 1])
            total = total + jnp.sum(jnp.where(hit, part, 0.0), axis=0, keepdims=True)
        if b + 1 == BUCKETS:
            total = total + far
        out = jnp.where(lane == b, jnp.sum(total, axis=1, keepdims=True), out)
    return out


class Rows:
    def __init__(self, ref, first, count):
        self.ref, self.first, self.count = ref, first, count

    def part(self, index):
        devices = 256 // self.count
        block = self.ref[
            pl.ds(index * devices, devices), self.first : self.first + self.count, :
        ]
        return block.reshape(256, 128)


def turn(rows, out_ref):
    for i in range(N * rows.count // 256):
        out_ref[:, i * 256 : i * 256 + 256] = rows.part(i).T


def left_half(rows, out_ref):
    left = left_lanes(256)
    for i in range(N * rows.count // 256):
        out_ref[i * 256 : i * 256 + 256, :] = jnp.where(left, rows.part(i), 0).astype(BF)


def query_out(grad_ref, out_ref, row):
    left = left_lanes(DROW // 2)
    for first in range(0, DEC, 256):
        part = grad_ref[:, first : first + 256].astype(BF)
        rows = jnp.concatenate([part, part], axis=0).T
        for i in range(256 // DROW):
            a = rows[i * DROW : i * DROW + DROW // 2]
            b = rows[i * DROW + DROW // 2 : (i + 1) * DROW]
            out_ref[first // DROW + i, row : row + DROW // 2] = jnp.where(left, a, b)


def finish_rows(high_sum, out_t, grad_t):
    inverse = 1.0 / high_sum
    out_t = out_t * inverse
    scaled = (grad_t.astype(F32) * inverse).astype(BF)
    delta = jnp.sum(scaled.astype(F32) * out_t, axis=0, keepdims=True)
    zero = jnp.zeros_like(scaled)
    rows = jnp.concatenate([zero, scaled], axis=0).T
    return scaled, delta, rows


def self_part(x1, x2, gs, bias_out, t1, t2, mk_s, mq, tiles, scores, e_s, sg, delta_ref, rq, rg, dq):
    turn(x1, t1)
    turn(x2, t2)
    zeros = jnp.zeros((HD, 256), BF)
    left_half(x1, rq)

    for tb in range(DEC // 256):
        span = slice(tb * 256, tb * 256 + 256)
        right = jnp.concatenate([zeros, t1[0:HD, span], mq[:, span]], axis=0)
        high = jnp.full((1, 256), -4.0 * BIG, F32)
        for cu in range(tb + 1):
            rows = slice(cu * 256, cu * 256 + 256)
            s = dot(jnp.concatenate([x1.part(cu), mk_s[rows, :]], axis=1), right)
            if tb - cu < 2:
                at = 256 * (1 - (tb - cu))
                s = s + tiles[at : at + 256, :]
            scores[rows, :] = s
            high = jnp.maximum(high, jnp.max(s, axis=0, keepdims=True))
        total = jnp.zeros((1, 256), F32)
        out_t = jnp.zeros((HD, 256), F32)
        for cu in range(tb + 1):
            rows = slice(cu * 256, cu * 256 + 256)
            e = jnp.exp(scores[rows, :] - high)
            total = total + jnp.sum(e, axis=0, keepdims=True)
            narrow = e.astype(BF)
            e_s[rows, span] = narrow
            out_t = out_t + dot(t2[0:HD, rows], narrow)
        scaled, delta, rows_g = finish_rows(total, out_t, t2[HD:128, span])
        sg[:, span] = scaled
        delta_ref[:, span] = delta
        rg[span, :] = rows_g

    near = jnp.zeros((128, 128), F32)
    next_one = jnp.zeros((128, 128), F32)
    far = jnp.zeros((1, 128), F32)
    dq[...] = jnp.zeros_like(dq)

    def fold(x):
        x = jnp.sum(x, axis=0, keepdims=True)
        return sum(x[:, i : i + 128] for i in range(0, x.shape[1], 128))

    for cu in range(DEC // 256):
        rows = slice(cu * 256, cu * 256 + 256)
        span = slice(cu * 256, DEC)
        width = DEC - cu * 256
        right = jnp.concatenate([sg[:, span], jnp.zeros((HD, width), BF)], axis=0)
        dp = dot(x2.part(cu), right)
        e = e_s[rows, span]
        ds = e.astype(F32) * (dp - delta_ref[:, span])
        narrow = ds.astype(BF)
        part = dot(narrow, rq[span, :]) + dot(e, rg[span, :])
        for i in range(256 // DROW):
            gs[cu * (256 // DROW) + i, 0:DROW] = part[i * DROW : (i + 1) * DROW].astype(BF)
        dq[:, span] += dot(t1[HD:128, rows], narrow)
        near = near + ds[0:128, 0:128] + ds[128:256, 128:256]
        next_one = next_one + ds[0:128, 128:256]
        if width > 256:
            next_one = next_one + ds[128:256, 256:384]
            far = far + fold(ds[0:128, 256:]) + fold(ds[128:256, 384:])
    bias_out[...] = bucket_sums(near, next_one, far)


def cross_rows(x4, t3, t4, mk_c, mq, scores, e_c, sg, delta_ref, rg):
    def block(tb, carry):
        span = pl.ds(pl.multiple_of(tb * 256, 256), 256)
        right = jnp.concatenate([t3[0:HD, span], jnp.zeros((HD, 256), BF), mq[:, span]], axis=0)
        high = jnp.full((1, 256), -4.0 * BIG, F32)
        for cu in range(ENC // 256):
            rows = slice(cu * 256, cu * 256 + 256)
            s = dot(jnp.concatenate([x4.part(cu), mk_c[rows, :]], axis=1), right)
            scores[rows, :] = s
            high = jnp.maximum(high, jnp.max(s, axis=0, keepdims=True))
        total = jnp.zeros((1, 256), F32)
        out_t = jnp.zeros((HD, 256), F32)
        for cu in range(ENC // 256):
            rows = slice(cu * 256, cu * 256 + 256)
            e = jnp.exp(scores[rows, :] - high)
            total = total + jnp.sum(e, axis=0, keepdims=True)
            narrow = e.astype(BF)
            e_c[rows, span] = narrow
            out_t = out_t + dot(t4[HD:128, rows], narrow)
        scaled, delta, rows_g = finish_rows(total, out_t, t3[HD:128, span])
        sg[:, span] = scaled
        delta_ref[:, span] = delta
        rg[span, :] = rows_g
        return carry

    lax.fori_loop(0, DEC // 256, block, 0)


def cross_keys(first, count, xc, t4, g3, e_c, sg, delta_ref, rq, rg, dq):
    size = count * EROW
    rows = pl.ds(pl.multiple_of(first * EROW, EROW), size)
    right = jnp.concatenate([jnp.zeros((HD, DEC), BF), sg[...]], axis=0)
    dp = dot(xc[pl.ds(first, count), 0:EROW, :].reshape(size, 128), right)
    e = e_c[rows, :]
    narrow = (e.astype(F32) * (dp - delta_ref[...])).astype(BF)
    part = dot(narrow, rq[...]) + dot(e, rg[...])
    for i in range(count):
        g3[first + i] = part[i * EROW : (i + 1) * EROW].astype(BF)
    dq[...] += dot(t4[0:HD, rows], narrow)


def fused_kernel(
    q_s, k_s, v_s, g_s, q_c, k_c, v_c, g_c, dec_len, enc_len, rel_bias,
    r3, rs, rb,
    aq, ak, av, ag, bq, bk, bv, bg, dec_v, enc_v, rel_v,
    pc, ps, xc, xs, g3, gs, bias, dp_part, bias_sum,
    t1, t2, t3, t4, mk_s, mk_c, mq, tiles, scores, e_s, e_c, sg, delta_ref, rq, rg, dq,
    in_sem, send_sem, recv_sem, dp_sem, up_sem, down_sem, dp_in,
):
    me, z, c = place()
    my_dp = lax.axis_index("dp")
    greet_near()
    loads = []
    pairs = (
        (k_c, bk), (v_c, bv), (q_c, bq), (g_c, bg), (q_s, aq), (k_s, ak), (v_s, av), (g_s, ag),
        (dec_len, dec_v), (enc_len, enc_v), (rel_bias, rel_v),
    )
    for i, (src, dst) in enumerate(pairs):
        load = pltpu.make_async_copy(src, dst, in_sem.at[i])
        load.start()
        loads.append(load)

    def send_all(which, src, dst, steps):
        copies = []
        for step in steps:
            copy = seq_copy(
                src.at[target_of(*step)], dst.at[me], send_sem, recv_sem, which, step
            )
            copy.start()
            copies.append(copy)
        return copies

    for load in loads[:4]:
        load.wait()
    pack_heads(bk, bv, pc, 0)
    pack_heads(bq, bg, pc, EROW)
    wait_near()
    pass_on(up_sem, down_sem, 2)
    tell(dp_in, dp_peer(1))
    in_c = send_all(0, pc, xc, NEAR)
    for hops in (2, 3, 4):
        heard(up_sem, down_sem, hops)
        if hops < 4:
            pass_on(up_sem, down_sem, hops + 1)
        in_c += send_all(0, pc, xc, at_hops(hops))
    pl.semaphore_wait(dp_in, 1)
    for load in loads[4:]:
        load.wait()
    pack_heads(aq, ak, ps, 0)
    pack_heads(av, ag, ps, DROW)
    xc[me] = pc[me]
    xs[me] = ps[me]
    dec_low, dec_high, dec_low_c, dec_high_c = bounds_of(dec_v)
    enc_low, enc_high, unused_low, unused_high = bounds_of(enc_v)
    key_features(dec_low, dec_high, mk_s, DEC)
    in_s = send_all(1, ps, xs, STEPS)
    key_features(enc_low, enc_high, mk_c, ENC)
    query_features(dec_low_c, dec_high_c, mq)
    bias_tiles(rel_v, me, tiles)
    x1, x2 = Rows(xs, 0, DROW), Rows(xs, DROW, DROW)
    x3, x4 = Rows(xc, EROW, DROW), Rows(xc, 0, EROW)

    left = left_lanes(2 * DROW)
    for dz in (0, 1, 7, 2, 6, 3, 5, 4):
        for copy, step in zip(in_c, IN_ORDER):
            if step[0] == dz:
                copy.wait_recv()
        chip = lax.rem(z + N // 2 - dz, N // 2)
        block = xc[pl.ds(2 * chip, 2), 0:EROW, :].reshape(2 * EROW, 128)
        t4[:, pl.ds(pl.multiple_of(chip * 2 * EROW, 2 * EROW), 2 * EROW)] = block.T
        block = xc[pl.ds(2 * chip, 2), EROW : EROW + DROW, :].reshape(2 * DROW, 128)
        first = pl.multiple_of(chip * 2 * DROW, 2 * DROW)
        t3[:, pl.ds(first, 2 * DROW)] = block.T
        rq[pl.ds(first, 2 * DROW), :] = jnp.where(left, block, 0).astype(BF)
    cross_rows(x4, t3, t4, mk_c, mq, scores, e_c, sg, delta_ref, rg)
    dq[...] = jnp.zeros_like(dq)
    out3, ready = [], []

    for dz in (4, 3, 5, 2, 6, 1, 7, 0):
        chip = lax.rem(z + dz, N // 2)
        for first, count in ((0, 1), (1, 1)) if dz == 4 else ((0, 2),):
            cross_keys(
                2 * chip + first, count, xc, t4, g3, e_c, sg, delta_ref, rq, rg, dq
            )
            out3 += send_all(2, g3, r3, ready)
            if count == 1:
                ready = [(dz, lax.rem(c + first, 2))]
            else:
                ready = [(dz, dc) for dc in (0, 1) if (dz, dc) != (0, 0)]
    query_out(dq, gs, DROW + DROW // 2)
    out3 += send_all(2, g3, r3, ready)
    r3[me] = g3[me]

    for copy in in_s:
        copy.wait_recv()
    self_part(x1, x2, gs, bias, t1, t2, mk_s, mq, tiles, scores, e_s, sg, delta_ref, rq, rg, dq)
    dp_copies = []
    for k in range(1, 4):
        copy = pltpu.make_async_remote_copy(
            src_ref=bias,
            dst_ref=dp_part.at[my_dp],
            send_sem=dp_sem.at[0, k],
            recv_sem=dp_sem.at[1, k],
            device_id=dp_peer(k),
            device_id_type=pl.DeviceIdType.MESH,
        )
        copy.start()
        dp_copies.append(copy)
    dp_part[my_dp] = bias[...]
    query_out(dq, gs, DROW)
    out_s = send_all(3, gs, rs, STEPS[:4])
    rs[me] = gs[me]
    for copy in dp_copies:
        copy.wait()
    total = ((dp_part[0] + dp_part[1]) + dp_part[2]) + dp_part[3]
    bias_sum[...] = total
    rb[me] = total
    out_s += send_all(3, gs, rs, STEPS[4:6])
    for step in STEPS:
        copy = seq_copy(bias_sum, rb.at[me], send_sem, recv_sem, 4, step)
        copy.start()
        out_s.append(copy)
    out_s += send_all(3, gs, rs, STEPS[6:])
    for copy in in_c + in_s:
        copy.wait_send()
    for copy in out3 + out_s:
        copy.wait()


def fused(*arrays):
    vm = pltpu.VMEM
    return pl.pallas_call(
        fused_kernel,
        out_shape=[
            jax.ShapeDtypeStruct((N, EROW, 128), BF),
            jax.ShapeDtypeStruct((N, EROW, 128), BF),
            jax.ShapeDtypeStruct((N, 1, 128), F32),
        ],
        in_specs=[pl.BlockSpec(memory_space=pltpu.HBM)] * 11,
        out_specs=[VM] * 3,
        scratch_shapes=[
            *[vm((DROW, N * HD), BF)] * 5,
            *[vm((EROW, N * HD), BF)] * 2,
            vm((DROW, N * HD), BF),
            vm((1, NEX), jnp.int32),
            vm((1, NEX), jnp.int32),
            vm((N, BUCKETS), F32),
            vm((N, EROW + DROW, 128), BF),
            vm((N, 2 * DROW, 128), BF),
            vm((N, EROW + DROW, 128), BF),
            vm((N, 2 * DROW, 128), BF),
            vm((N, EROW, 128), BF),
            vm((N, 2 * DROW, 128), BF),
            vm((1, 128), F32),
            vm((4, 1, 128), F32),
            vm((1, 128), F32),
            *[vm((128, DEC), BF)] * 3,
            vm((128, ENC), BF),
            vm((DEC, 128), BF),
            vm((ENC, 128), BF),
            vm((128, DEC), BF),
            vm((512, 256), F32),
            vm((ENC, 256), F32),
            vm((DEC, DEC), BF),
            vm((ENC, DEC), BF),
            vm((HD, DEC), BF),
            vm((1, DEC), F32),
            vm((DEC, 128), BF),
            vm((DEC, 128), BF),
            vm((HD, DEC), F32),
            pltpu.SemaphoreType.DMA((11,)),
            pltpu.SemaphoreType.DMA((5, N)),
            pltpu.SemaphoreType.DMA((5, N)),
            pltpu.SemaphoreType.DMA((2, 4)),
            pltpu.SemaphoreType.REGULAR((5,)),
            pltpu.SemaphoreType.REGULAR((5,)),
            pltpu.SemaphoreType.REGULAR,
        ],
        compiler_params=pltpu.CompilerParams(collective_id=0, has_side_effects=True, vmem_limit_bytes=32 * 1024 * 1024
        ),
        name="attention_grads",
    )(*arrays)


def on_device(q_s, k_s, v_s, g_s, q_c, k_c, v_c, g_c, dec_len, enc_len, rel_bias):
    flat = [x.reshape(x.shape[1], x.shape[2]) for x in (q_s, k_s, v_s, g_s, q_c, k_c, v_c, g_c)]
    operands = [
        pltpu.with_memory_space_constraint(x, pltpu.HBM)
        for x in (*flat, dec_len, enc_len, rel_bias.T)
    ]
    outs = unpack(*fused(*operands))
    return tuple(x.reshape((1,) + x.shape) for x in outs[:6]) + (outs[6].T,)


def solution(mesh):
    rows = P("dp", "seq", "mp")
    return jax.shard_map(
        on_device,
        mesh=mesh,
        in_specs=(rows,) * 8 + (P("dp", None), P("dp", None), P(None, "mp")),
        out_specs=(rows,) * 6 + (P(None, "mp"),),
        check_vma=False,
    )
```

```python
import functools
import math

import jax
import jax.numpy as jnp
from jax import lax
from jax.experimental import pallas as pl
from jax.experimental.pallas import tpu as pltpu
from jax.sharding import PartitionSpec as P

HD = 64
BUCKETS = 32
DISTANCE = 128
NEX = 16
N = 16
DEC = 1024
ENC = 2048
DROW = DEC // N
EROW = ENC // N
BIG = 131072.0
BF = jnp.bfloat16
F32 = jnp.float32
VM = pl.BlockSpec(memory_space=pltpu.VMEM)

STEPS = [
    (dz, dc)
    for dz in (3, 5, 4, 2, 6, 1, 7, 0)
    for dc in (0, 1)
    if (dz, dc) != (0, 0)
]


def thresholds():
    half = BUCKETS // 2
    lows = list(range(half + 1))
    for level in range(1, BUCKETS - half):
        lows.append(math.ceil(half * (DISTANCE / half) ** (level / (BUCKETS - half))))
    return lows


LOWS = thresholds()


def swap_halves(x):
    return jnp.concatenate([x[:, HD:], x[:, :HD]], axis=1)


def left_lanes(rows):
    return lax.broadcasted_iota(jnp.int32, (rows, 128), 1) < HD


def dot(a, b):
    return jnp.dot(a, b, preferred_element_type=F32)


def place():
    me = lax.axis_index("seq")
    return me, lax.div(me, 2), lax.rem(me, 2)


def target_of(dz, dc):
    me, z, c = place()
    return lax.rem(z + dz, N // 2) * 2 + lax.rem(c + dc, 2)


def tell(semaphore, device):
    pl.semaphore_signal(
        semaphore, inc=1, device_id=device, device_id_type=pl.DeviceIdType.MESH
    )


def dp_peer(shift):
    return {"dp": lax.rem(lax.axis_index("dp") + shift, 4)}


NEAR = [step for step in STEPS if step[0] in (0, 1, N // 2 - 1)]


def at_hops(hops):
    return [step for step in STEPS if step[0] in (hops, N // 2 - hops)]


IN_ORDER = NEAR + at_hops(2) + at_hops(3) + at_hops(4)


def greet_near():
    barrier = pltpu.get_barrier_semaphore()
    for step in NEAR:
        tell(barrier, {"seq": target_of(*step)})
    tell(barrier, dp_peer(1))
    tell(barrier, dp_peer(3))


def wait_near():
    pl.semaphore_wait(pltpu.get_barrier_semaphore(), len(NEAR) + 2)


def pass_on(up_sem, down_sem, hops):
    tell(up_sem.at[hops], {"seq": target_of(1, 0)})
    tell(down_sem.at[hops], {"seq": target_of(N // 2 - 1, 0)})


def heard(up_sem, down_sem, hops):
    pl.semaphore_wait(up_sem.at[hops], 1)
    pl.semaphore_wait(down_sem.at[hops], 1)


def seq_copy(src, dst, send_sem, recv_sem, which, step):
    dz, dc = step
    return pltpu.make_async_remote_copy(
        src_ref=src,
        dst_ref=dst,
        send_sem=send_sem.at[which, dz * 2 + dc],
        recv_sem=recv_sem.at[which, dz * 2 + dc],
        device_id={"seq": target_of(dz, dc)},
        device_id_type=pl.DeviceIdType.MESH,
    )


def pack_heads(a_ref, b_ref, out_ref, first):
    rows = a_ref.shape[0]
    left = left_lanes(rows)
    span = slice(first, first + rows)
    for pair in range(N // 2):
        a = a_ref[:, pair * 128 : pair * 128 + 128]
        b = b_ref[:, pair * 128 : pair * 128 + 128]
        out_ref[2 * pair, span] = jnp.where(left, a, swap_halves(b))
        out_ref[2 * pair + 1, span] = jnp.where(left, swap_halves(a), b)


def unpack_chip(src, chip, first, rows, left_out, left_row, right_out, right_row):
    left = left_lanes(rows)
    span = slice(first, first + rows)
    a, b = src[2 * chip, span], src[2 * chip + 1, span]
    lanes = pl.ds(pl.multiple_of(chip * 128, 128), 128)
    left_out[left_row : left_row + rows, lanes] = jnp.where(left, a, swap_halves(b))
    right_out[right_row : right_row + rows, lanes] = jnp.where(left, swap_halves(a), b)


OUT_SHAPES = [jax.ShapeDtypeStruct((DROW, N * HD), BF)] * 4 + [
    jax.ShapeDtypeStruct((EROW, N * HD), BF),
    jax.ShapeDtypeStruct((EROW, N * HD), BF),
    jax.ShapeDtypeStruct((N, BUCKETS), F32),
]


def leave_kernel(*refs):
    made, outs, sems = refs[:7], refs[7:14], refs[14]
    copies = [pltpu.make_async_copy(made[i], outs[i], sems.at[i]) for i in range(7)]
    for copy in copies:
        copy.start()
    for copy in copies:
        copy.wait()


def leave(*arrays):
    return pl.pallas_call(
        leave_kernel,
        out_shape=OUT_SHAPES,
        in_specs=[VM] * 7,
        out_specs=[pl.BlockSpec(memory_space=pl.ANY)] * 7,
        scratch_shapes=[pltpu.SemaphoreType.DMA((7,))],
        compiler_params=pltpu.CompilerParams(vmem_limit_bytes=16 * 1024 * 1024),
        name="leave",
    )(*arrays)


def iota(shape, axis):
    return lax.broadcasted_iota(jnp.int32, shape, axis)


def bounds_of(length_ref):
    row = jnp.concatenate(
        [length_ref[...].astype(F32), jnp.zeros((1, 128 - NEX), F32)], axis=1
    )
    spread = jnp.broadcast_to(row, (128, 128))
    sub, lane = iota((128, 128), 0), iota((128, 128), 1)
    turned = spread.T
    low_row = jnp.sum(jnp.where(sub < lane, turned, 0.0), axis=0, keepdims=True)
    high_row = jnp.sum(jnp.where(sub <= lane, turned, 0.0), axis=0, keepdims=True)
    low_col = jnp.sum(jnp.where(lane < sub, spread, 0.0), axis=1, keepdims=True)
    high_col = jnp.sum(jnp.where(lane <= sub, spread, 0.0), axis=1, keepdims=True)
    return low_row, high_row, low_col[:NEX], high_col[:NEX]


def key_features(low, high, out_ref, rows):
    low, high = low.astype(jnp.int32), high.astype(jnp.int32)
    for first in range(0, rows, 256):
        row = iota((256, 128), 0) + first
        inside = (row >= low) & (row < high)
        out_ref[first : first + 256, :] = jnp.where(inside, 1.0, 0.0).astype(BF)


def query_features(low, high, out_ref):
    col = iota((NEX, DEC), 1)
    inside = (col >= low.astype(jnp.int32)) & (col < high.astype(jnp.int32))
    out_ref[0:NEX, :] = jnp.where(inside, 0.0, -BIG).astype(BF)
    out_ref[NEX:128, :] = jnp.zeros((128 - NEX, DEC), BF)


def bias_tiles(rel_bias, head, tile_ref):
    base = lax.broadcasted_iota(jnp.int32, (128, 128), 1) - lax.broadcasted_iota(
        jnp.int32, (128, 128), 0
    )
    row = iota((N, BUCKETS), 0)
    table = jnp.sum(jnp.where(row == head, rel_bias[...], 0.0), axis=0, keepdims=True)
    table = table - table[:, BUCKETS - 1 :]
    made = []
    for shift in (0, 128):
        distance = base + shift
        tile = jnp.broadcast_to(table[:, 0:1], (128, 128))
        for b in range(1, BUCKETS):
            tile = jnp.where(distance >= LOWS[b], table[:, b : b + 1], tile)
        made.append(jnp.where(distance >= 0, tile, -BIG))
    near, next_one = made
    zero = jnp.zeros((128, 128), F32)
    tile_ref[0:128, 0:128] = zero
    tile_ref[0:128, 128:256] = zero
    tile_ref[128:256, 0:128] = next_one
    tile_ref[128:256, 128:256] = zero
    tile_ref[256:384, 0:128] = near
    tile_ref[256:384, 128:256] = next_one
    tile_ref[384:512, 0:128] = jnp.full((128, 128), -BIG, F32)
    tile_ref[384:512, 128:256] = near


def bucket_sums(near, next_one, far):
    base = lax.broadcasted_iota(jnp.int32, (128, 128), 1) - lax.broadcasted_iota(
        jnp.int32, (128, 128), 0
    )
    lane = lax.broadcasted_iota(jnp.int32, (1, 128), 1)
    out = jnp.zeros((1, 128), F32)
    for b in range(BUCKETS):
        total = jnp.zeros((1, 128), F32)
        for shift, part in ((0, near), (128, next_one)):
            distance = base + shift
            hit = distance >= LOWS[b]
            if b + 1 < BUCKETS:
                hit = hit & (distance < LOWS[b + 1])
            total = total + jnp.sum(jnp.where(hit, part, 0.0), axis=0, keepdims=True)
        if b + 1 == BUCKETS:
            total = total + far
        out = jnp.where(lane == b, jnp.sum(total, axis=1, keepdims=True), out)
    return out


class Rows:
    def __init__(self, ref, first, count):
        self.ref, self.first, self.count = ref, first, count

    def part(self, index):
        devices = 256 // self.count
        block = self.ref[
            pl.ds(index * devices, devices), self.first : self.first + self.count, :
        ]
        return block.reshape(256, 128)


def turn(rows, out_ref):
    for i in range(N * rows.count // 256):
        out_ref[:, i * 256 : i * 256 + 256] = rows.part(i).T


def left_half(rows, out_ref):
    left = left_lanes(256)
    for i in range(N * rows.count // 256):
        out_ref[i * 256 : i * 256 + 256, :] = jnp.where(left, rows.part(i), 0).astype(BF)


def query_out(grad_ref, out_ref, row):
    left = left_lanes(DROW // 2)
    for first in range(0, DEC, 256):
        part = grad_ref[:, first : first + 256].astype(BF)
        rows = jnp.concatenate([part, part], axis=0).T
        for i in range(256 // DROW):
            a = rows[i * DROW : i * DROW + DROW // 2]
            b = rows[i * DROW + DROW // 2 : (i + 1) * DROW]
            out_ref[first // DROW + i, row : row + DROW // 2] = jnp.where(left, a, b)


def finish_rows(high_sum, out_t, grad_t):
    inverse = 1.0 / high_sum
    out_t = out_t * inverse
    scaled = (grad_t.astype(F32) * inverse).astype(BF)
    delta = jnp.sum(scaled.astype(F32) * out_t, axis=0, keepdims=True)
    zero = jnp.zeros_like(scaled)
    rows = jnp.concatenate([zero, scaled], axis=0).T
    return scaled, delta, rows


def self_part(x1, x2, gs, bias_out, t1, t2, mk_s, mq, tiles, scores, e_s, sg, delta_ref, rq, rg, dq):
    turn(x1, t1)
    turn(x2, t2)
    zeros = jnp.zeros((HD, 256), BF)
    left_half(x1, rq)

    for tb in range(DEC // 256):
        span = slice(tb * 256, tb * 256 + 256)
        right = jnp.concatenate([zeros, t1[0:HD, span], mq[:, span]], axis=0)
        high = jnp.full((1, 256), -4.0 * BIG, F32)
        for cu in range(tb + 1):
            rows = slice(cu * 256, cu * 256 + 256)
            s = dot(jnp.concatenate([x1.part(cu), mk_s[rows, :]], axis=1), right)
            if tb - cu < 2:
                at = 256 * (1 - (tb - cu))
                s = s + tiles[at : at + 256, :]
            scores[rows, :] = s
            high = jnp.maximum(high, jnp.max(s, axis=0, keepdims=True))
        total = jnp.zeros((1, 256), F32)
        out_t = jnp.zeros((HD, 256), F32)
        for cu in range(tb + 1):
            rows = slice(cu * 256, cu * 256 + 256)
            e = jnp.exp(scores[rows, :] - high)
            total = total + jnp.sum(e, axis=0, keepdims=True)
            narrow = e.astype(BF)
            e_s[rows, span] = narrow
            out_t = out_t + dot(t2[0:HD, rows], narrow)
        scaled, delta, rows_g = finish_rows(total, out_t, t2[HD:128, span])
        sg[:, span] = scaled
        delta_ref[:, span] = delta
        rg[span, :] = rows_g

    near = jnp.zeros((128, 128), F32)
    next_one = jnp.zeros((128, 128), F32)
    far = jnp.zeros((1, 128), F32)
    dq[...] = jnp.zeros_like(dq)

    def fold(x):
        x = jnp.sum(x, axis=0, keepdims=True)
        return sum(x[:, i : i + 128] for i in range(0, x.shape[1], 128))

    for cu in range(DEC // 256):
        rows = slice(cu * 256, cu * 256 + 256)
        span = slice(cu * 256, DEC)
        width = DEC - cu * 256
        right = jnp.concatenate([sg[:, span], jnp.zeros((HD, width), BF)], axis=0)
        dp = dot(x2.part(cu), right)
        e = e_s[rows, span]
        ds = e.astype(F32) * (dp - delta_ref[:, span])
        narrow = ds.astype(BF)
        part = dot(narrow, rq[span, :]) + dot(e, rg[span, :])
        for i in range(256 // DROW):
            gs[cu * (256 // DROW) + i, 0:DROW] = part[i * DROW : (i + 1) * DROW].astype(BF)
        dq[:, span] += dot(t1[HD:128, rows], narrow)
        near = near + ds[0:128, 0:128] + ds[128:256, 128:256]
        next_one = next_one + ds[0:128, 128:256]
        if width > 256:
            next_one = next_one + ds[128:256, 256:384]
            far = far + fold(ds[0:128, 256:]) + fold(ds[128:256, 384:])
    bias_out[...] = bucket_sums(near, next_one, far)


def cross_rows(x4, t3, t4, mk_c, mq, scores, e_c, sg, delta_ref, rg):
    def block(tb, carry):
        span = pl.ds(pl.multiple_of(tb * 256, 256), 256)
        right = jnp.concatenate([t3[0:HD, span], jnp.zeros((HD, 256), BF), mq[:, span]], axis=0)
        high = jnp.full((1, 256), -4.0 * BIG, F32)
        for cu in range(ENC // 256):
            rows = slice(cu * 256, cu * 256 + 256)
            s = dot(jnp.concatenate([x4.part(cu), mk_c[rows, :]], axis=1), right)
            scores[rows, :] = s
            high = jnp.maximum(high, jnp.max(s, axis=0, keepdims=True))
        total = jnp.zeros((1, 256), F32)
        out_t = jnp.zeros((HD, 256), F32)
        for cu in range(ENC // 256):
            rows = slice(cu * 256, cu * 256 + 256)
            e = jnp.exp(scores[rows, :] - high)
            total = total + jnp.sum(e, axis=0, keepdims=True)
            narrow = e.astype(BF)
            e_c[rows, span] = narrow
            out_t = out_t + dot(t4[HD:128, rows], narrow)
        scaled, delta, rows_g = finish_rows(total, out_t, t3[HD:128, span])
        sg[:, span] = scaled
        delta_ref[:, span] = delta
        rg[span, :] = rows_g
        return carry

    lax.fori_loop(0, DEC // 256, block, 0)


def cross_keys(first, count, xc, t4, g3, e_c, sg, delta_ref, rq, rg, dq):
    size = count * EROW
    rows = pl.ds(pl.multiple_of(first * EROW, EROW), size)
    right = jnp.concatenate([jnp.zeros((HD, DEC), BF), sg[...]], axis=0)
    dp = dot(xc[pl.ds(first, count), 0:EROW, :].reshape(size, 128), right)
    e = e_c[rows, :]
    narrow = (e.astype(F32) * (dp - delta_ref[...])).astype(BF)
    part = dot(narrow, rq[...]) + dot(e, rg[...])
    for i in range(count):
        g3[first + i] = part[i * EROW : (i + 1) * EROW].astype(BF)
    dq[...] += dot(t4[0:HD, rows], narrow)


def fused_kernel(
    q_s, k_s, v_s, g_s, q_c, k_c, v_c, g_c, dec_len, enc_len, rel_bias,
    dqs, dks, dvs, dqc, dkc, dvc, dbias,
    aq, ak, av, ag, bq, bk, bv, bg, dec_v, enc_v, rel_v,
    pc, ps, xc, xs, g3, gs, r3, rs, rb, bias, dp_part, bias_sum,
    t1, t2, t3, t4, mk_s, mk_c, mq, tiles, scores, e_s, e_c, sg, delta_ref, rq, rg, dq,
    in_sem, send_sem, recv_sem, dp_sem, up_sem, down_sem, dp_in,
):
    me, z, c = place()
    my_dp = lax.axis_index("dp")
    greet_near()
    loads = []
    pairs = (
        (k_c, bk), (v_c, bv), (q_c, bq), (g_c, bg), (q_s, aq), (k_s, ak), (v_s, av), (g_s, ag),
        (dec_len, dec_v), (enc_len, enc_v), (rel_bias, rel_v),
    )
    for i, (src, dst) in enumerate(pairs):
        load = pltpu.make_async_copy(src, dst, in_sem.at[i])
        load.start()
        loads.append(load)

    def send_all(which, src, dst, steps):
        copies = []
        for step in steps:
            copy = seq_copy(
                src.at[target_of(*step)], dst.at[me], send_sem, recv_sem, which, step
            )
            copy.start()
            copies.append(copy)
        return copies

    for load in loads[:4]:
        load.wait()
    pack_heads(bk, bv, pc, 0)
    pack_heads(bq, bg, pc, EROW)
    wait_near()
    pass_on(up_sem, down_sem, 2)
    tell(dp_in, dp_peer(1))
    in_c = send_all(0, pc, xc, NEAR)
    for hops in (2, 3, 4):
        heard(up_sem, down_sem, hops)
        if hops < 4:
            pass_on(up_sem, down_sem, hops + 1)
        in_c += send_all(0, pc, xc, at_hops(hops))
    pl.semaphore_wait(dp_in, 1)
    for load in loads[4:]:
        load.wait()
    pack_heads(aq, ak, ps, 0)
    pack_heads(av, ag, ps, DROW)
    xc[me] = pc[me]
    xs[me] = ps[me]
    dec_low, dec_high, dec_low_c, dec_high_c = bounds_of(dec_v)
    enc_low, enc_high, unused_low, unused_high = bounds_of(enc_v)
    key_features(dec_low, dec_high, mk_s, DEC)
    in_s = send_all(1, ps, xs, STEPS)
    key_features(enc_low, enc_high, mk_c, ENC)
    query_features(dec_low_c, dec_high_c, mq)
    bias_tiles(rel_v, me, tiles)
    x1, x2 = Rows(xs, 0, DROW), Rows(xs, DROW, DROW)
    x3, x4 = Rows(xc, EROW, DROW), Rows(xc, 0, EROW)

    left = left_lanes(2 * DROW)
    for dz in (0, 1, 7, 2, 6, 3, 5, 4):
        for copy, step in zip(in_c, IN_ORDER):
            if step[0] == dz:
                copy.wait_recv()
        chip = lax.rem(z + N // 2 - dz, N // 2)
        block = xc[pl.ds(2 * chip, 2), 0:EROW, :].reshape(2 * EROW, 128)
        t4[:, pl.ds(pl.multiple_of(chip * 2 * EROW, 2 * EROW), 2 * EROW)] = block.T
        block = xc[pl.ds(2 * chip, 2), EROW : EROW + DROW, :].reshape(2 * DROW, 128)
        first = pl.multiple_of(chip * 2 * DROW, 2 * DROW)
        t3[:, pl.ds(first, 2 * DROW)] = block.T
        rq[pl.ds(first, 2 * DROW), :] = jnp.where(left, block, 0).astype(BF)
    cross_rows(x4, t3, t4, mk_c, mq, scores, e_c, sg, delta_ref, rg)
    dq[...] = jnp.zeros_like(dq)
    out3, ready = [], []

    for dz in (4, 3, 5, 2, 6, 1, 7, 0):
        chip = lax.rem(z + dz, N // 2)
        for first, count in ((0, 1), (1, 1)) if dz == 4 else ((0, 2),):
            cross_keys(
                2 * chip + first, count, xc, t4, g3, e_c, sg, delta_ref, rq, rg, dq
            )
            out3 += send_all(2, g3, r3, ready)
            if count == 1:
                ready = [(dz, lax.rem(c + first, 2))]
            else:
                ready = [(dz, dc) for dc in (0, 1) if (dz, dc) != (0, 0)]
    query_out(dq, gs, DROW + DROW // 2)
    out3 += send_all(2, g3, r3, ready)
    r3[me] = g3[me]

    for copy in in_s:
        copy.wait_recv()
    self_part(x1, x2, gs, bias, t1, t2, mk_s, mq, tiles, scores, e_s, sg, delta_ref, rq, rg, dq)
    dp_copies = []
    for k in range(1, 4):
        copy = pltpu.make_async_remote_copy(
            src_ref=bias,
            dst_ref=dp_part.at[my_dp],
            send_sem=dp_sem.at[0, k],
            recv_sem=dp_sem.at[1, k],
            device_id=dp_peer(k),
            device_id_type=pl.DeviceIdType.MESH,
        )
        copy.start()
        dp_copies.append(copy)
    dp_part[my_dp] = bias[...]
    query_out(dq, gs, DROW)
    out_s = send_all(3, gs, rs, IN_ORDER[:6])
    rs[me] = gs[me]
    for copy in dp_copies:
        copy.wait()
    total = ((dp_part[0] + dp_part[1]) + dp_part[2]) + dp_part[3]
    bias_sum[...] = total
    rb[me] = total
    out_s += send_all(3, gs, rs, IN_ORDER[6:8])
    out_b = []
    for step in STEPS:
        copy = seq_copy(bias_sum, rb.at[me], send_sem, recv_sem, 4, step)
        copy.start()
        out_b.append(copy)
    out_s += send_all(3, gs, rs, IN_ORDER[8:])
    half = DROW // 2
    for i, dz in enumerate((4, 3, 5, 2, 6, 1, 7, 0)):
        for copy in out3[2 * i : 2 * i + 2]:
            copy.wait_recv()
        chip = lax.rem(z + N // 2 - dz, N // 2)
        unpack_chip(r3, chip, 0, EROW, dkc, 0, dvc, 0)
    for copy in in_c + in_s + out3:
        copy.wait_send()
    for copy in out_b:
        copy.wait()
    rows = jnp.concatenate([rb[i] for i in range(N)], axis=0)
    dbias[...] = rows[:, :BUCKETS] * (1.0 / math.sqrt(4 * DEC))
    for dz in (0, 1, 7, 2, 6, 3, 5, 4):
        for copy, step in zip(out_s, IN_ORDER):
            if step[0] == dz:
                copy.wait_recv()
        chip = lax.rem(z + N // 2 - dz, N // 2)
        unpack_chip(rs, chip, 0, DROW, dks, 0, dvs, 0)
        unpack_chip(rs, chip, DROW, half, dqs, 0, dqs, half)
        unpack_chip(rs, chip, DROW + half, half, dqc, 0, dqc, half)
    for copy in out_s:
        copy.wait_send()


def fused(*arrays):
    vm = pltpu.VMEM
    return pl.pallas_call(
        fused_kernel,
        out_shape=OUT_SHAPES,
        in_specs=[pl.BlockSpec(memory_space=pltpu.HBM)] * 11,
        out_specs=[VM] * 7,
        scratch_shapes=[
            *[vm((DROW, N * HD), BF)] * 5,
            *[vm((EROW, N * HD), BF)] * 2,
            vm((DROW, N * HD), BF),
            vm((1, NEX), jnp.int32),
            vm((1, NEX), jnp.int32),
            vm((N, BUCKETS), F32),
            vm((N, EROW + DROW, 128), BF),
            vm((N, 2 * DROW, 128), BF),
            vm((N, EROW + DROW, 128), BF),
            vm((N, 2 * DROW, 128), BF),
            *[vm((N, EROW, 128), BF)] * 4,
            vm((N, 1, 128), F32),
            vm((1, 128), F32),
            vm((4, 1, 128), F32),
            vm((1, 128), F32),
            *[vm((128, DEC), BF)] * 3,
            vm((128, ENC), BF),
            vm((DEC, 128), BF),
            vm((ENC, 128), BF),
            vm((128, DEC), BF),
            vm((512, 256), F32),
            vm((ENC, 256), F32),
            vm((DEC, DEC), BF),
            vm((ENC, DEC), BF),
            vm((HD, DEC), BF),
            vm((1, DEC), F32),
            vm((DEC, 128), BF),
            vm((DEC, 128), BF),
            vm((HD, DEC), F32),
            pltpu.SemaphoreType.DMA((11,)),
            pltpu.SemaphoreType.DMA((5, N)),
            pltpu.SemaphoreType.DMA((5, N)),
            pltpu.SemaphoreType.DMA((2, 4)),
            pltpu.SemaphoreType.REGULAR((5,)),
            pltpu.SemaphoreType.REGULAR((5,)),
            pltpu.SemaphoreType.REGULAR,
        ],
        compiler_params=pltpu.CompilerParams(collective_id=0, has_side_effects=True, vmem_limit_bytes=32 * 1024 * 1024
        ),
        name="attention_grads",
    )(*arrays)


def on_device(q_s, k_s, v_s, g_s, q_c, k_c, v_c, g_c, dec_len, enc_len, rel_bias):
    flat = [x.reshape(x.shape[1], x.shape[2]) for x in (q_s, k_s, v_s, g_s, q_c, k_c, v_c, g_c)]
    operands = [
        pltpu.with_memory_space_constraint(x, pltpu.HBM)
        for x in (*flat, dec_len, enc_len, rel_bias.T)
    ]
    outs = leave(*fused(*operands))
    return tuple(x.reshape((1,) + x.shape) for x in outs[:6]) + (outs[6].T,)


def solution(mesh):
    rows = P("dp", "seq", "mp")
    return jax.shard_map(
        on_device,
        mesh=mesh,
        in_specs=(rows,) * 8 + (P("dp", None), P("dp", None), P(None, "mp")),
        out_specs=(rows,) * 6 + (P(None, "mp"),),
        check_vma=False,
    )
```

```python
import functools
import math

import jax
import jax.numpy as jnp
from jax import lax
from jax.experimental import pallas as pl
from jax.experimental.pallas import tpu as pltpu
from jax.sharding import PartitionSpec as P

HD = 64
BUCKETS = 32
DISTANCE = 128
NEX = 16
N = 16
DEC = 1024
ENC = 2048
DROW = DEC // N
EROW = ENC // N
BIG = 131072.0
BF = jnp.bfloat16
F32 = jnp.float32
VM = pl.BlockSpec(memory_space=pltpu.VMEM)

STEPS = [
    (dz, dc)
    for dz in (3, 5, 4, 2, 6, 1, 7, 0)
    for dc in (0, 1)
    if (dz, dc) != (0, 0)
]


def thresholds():
    half = BUCKETS // 2
    lows = list(range(half + 1))
    for level in range(1, BUCKETS - half):
        lows.append(math.ceil(half * (DISTANCE / half) ** (level / (BUCKETS - half))))
    return lows


LOWS = thresholds()


def swap_halves(x):
    return jnp.concatenate([x[:, HD:], x[:, :HD]], axis=1)


def left_lanes(rows):
    return lax.broadcasted_iota(jnp.int32, (rows, 128), 1) < HD


def dot(a, b):
    return jnp.dot(a, b, preferred_element_type=F32)


def place():
    me = lax.axis_index("seq")
    return me, lax.div(me, 2), lax.rem(me, 2)


def target_of(dz, dc):
    me, z, c = place()
    return lax.rem(z + dz, N // 2) * 2 + lax.rem(c + dc, 2)


def tell(semaphore, device):
    pl.semaphore_signal(
        semaphore, inc=1, device_id=device, device_id_type=pl.DeviceIdType.MESH
    )


def dp_peer(shift):
    return {"dp": lax.rem(lax.axis_index("dp") + shift, 4)}


NEAR = [step for step in STEPS if step[0] in (0, 1, N // 2 - 1)]


def at_hops(hops):
    return [step for step in STEPS if step[0] in (hops, N // 2 - hops)]


IN_ORDER = NEAR + at_hops(2) + at_hops(3) + at_hops(4)


def greet_near():
    barrier = pltpu.get_barrier_semaphore()
    for step in NEAR:
        tell(barrier, {"seq": target_of(*step)})
    tell(barrier, dp_peer(1))
    tell(barrier, dp_peer(3))


def wait_near():
    pl.semaphore_wait(pltpu.get_barrier_semaphore(), len(NEAR) + 2)


def pass_on(up_sem, down_sem, hops):
    tell(up_sem.at[hops], {"seq": target_of(1, 0)})
    tell(down_sem.at[hops], {"seq": target_of(N // 2 - 1, 0)})


def heard(up_sem, down_sem, hops):
    pl.semaphore_wait(up_sem.at[hops], 1)
    pl.semaphore_wait(down_sem.at[hops], 1)


def seq_copy(src, dst, send_sem, recv_sem, which, step):
    dz, dc = step
    return pltpu.make_async_remote_copy(
        src_ref=src,
        dst_ref=dst,
        send_sem=send_sem.at[which, dz * 2 + dc],
        recv_sem=recv_sem.at[which, dz * 2 + dc],
        device_id={"seq": target_of(dz, dc)},
        device_id_type=pl.DeviceIdType.MESH,
    )


def pack_heads(a_ref, b_ref, out_ref, first):
    rows = a_ref.shape[0]
    left = left_lanes(rows)
    span = slice(first, first + rows)
    for pair in range(N // 2):
        a = a_ref[:, pair * 128 : pair * 128 + 128]
        b = b_ref[:, pair * 128 : pair * 128 + 128]
        out_ref[2 * pair, span] = jnp.where(left, a, swap_halves(b))
        out_ref[2 * pair + 1, span] = jnp.where(left, swap_halves(a), b)


def unpack_chip(src, chip, first, rows, left_out, left_row, right_out, right_row):
    left = left_lanes(rows)
    span = slice(first, first + rows)
    a, b = src[2 * chip, span], src[2 * chip + 1, span]
    lanes = pl.ds(pl.multiple_of(chip * 128, 128), 128)
    left_out[left_row : left_row + rows, lanes] = jnp.where(left, a, swap_halves(b))
    right_out[right_row : right_row + rows, lanes] = jnp.where(left, swap_halves(a), b)


OUT_SHAPES = [jax.ShapeDtypeStruct((DROW, N * HD), BF)] * 4 + [
    jax.ShapeDtypeStruct((EROW, N * HD), BF),
    jax.ShapeDtypeStruct((EROW, N * HD), BF),
    jax.ShapeDtypeStruct((N, BUCKETS), F32),
]


def leave_kernel(*refs):
    made, outs, sems = refs[:7], refs[7:14], refs[14]
    copies = []
    for i in (4, 5, 0, 1, 2, 3, 6):
        size = made[i].shape[0] // 2
        for j in range(2 if i < 6 else 1):
            span = slice(j * size, j * size + size) if i < 6 else slice(0, N)
            copies.append(
                pltpu.make_async_copy(made[i].at[span], outs[i].at[span], sems.at[i, j])
            )
    for copy in copies:
        copy.start()
    for copy in copies:
        copy.wait()


def leave(*arrays):
    return pl.pallas_call(
        leave_kernel,
        out_shape=OUT_SHAPES,
        in_specs=[VM] * 7,
        out_specs=[pl.BlockSpec(memory_space=pl.ANY)] * 7,
        scratch_shapes=[pltpu.SemaphoreType.DMA((7, 2))],
        compiler_params=pltpu.CompilerParams(vmem_limit_bytes=16 * 1024 * 1024),
        name="leave",
    )(*arrays)


def iota(shape, axis):
    return lax.broadcasted_iota(jnp.int32, shape, axis)


def bounds_of(length_ref):
    row = jnp.concatenate(
        [length_ref[...].astype(F32), jnp.zeros((1, 128 - NEX), F32)], axis=1
    )
    spread = jnp.broadcast_to(row, (128, 128))
    sub, lane = iota((128, 128), 0), iota((128, 128), 1)
    turned = spread.T
    low_row = jnp.sum(jnp.where(sub < lane, turned, 0.0), axis=0, keepdims=True)
    high_row = jnp.sum(jnp.where(sub <= lane, turned, 0.0), axis=0, keepdims=True)
    low_col = jnp.sum(jnp.where(lane < sub, spread, 0.0), axis=1, keepdims=True)
    high_col = jnp.sum(jnp.where(lane <= sub, spread, 0.0), axis=1, keepdims=True)
    return low_row, high_row, low_col[:NEX], high_col[:NEX]


def key_features(low, high, out_ref, rows):
    low, high = low.astype(jnp.int32), high.astype(jnp.int32)
    for first in range(0, rows, 256):
        row = iota((256, 128), 0) + first
        inside = (row >= low) & (row < high)
        out_ref[first : first + 256, :] = jnp.where(inside, 1.0, 0.0).astype(BF)


def query_features(low, high, out_ref):
    col = iota((NEX, DEC), 1)
    inside = (col >= low.astype(jnp.int32)) & (col < high.astype(jnp.int32))
    out_ref[0:NEX, :] = jnp.where(inside, 0.0, -BIG).astype(BF)
    out_ref[NEX:128, :] = jnp.zeros((128 - NEX, DEC), BF)


def bias_tiles(rel_bias, head, tile_ref):
    base = lax.broadcasted_iota(jnp.int32, (128, 128), 1) - lax.broadcasted_iota(
        jnp.int32, (128, 128), 0
    )
    row = iota((N, BUCKETS), 0)
    table = jnp.sum(jnp.where(row == head, rel_bias[...], 0.0), axis=0, keepdims=True)
    table = table - table[:, BUCKETS - 1 :]
    made = []
    for shift in (0, 128):
        distance = base + shift
        tile = jnp.broadcast_to(table[:, 0:1], (128, 128))
        for b in range(1, BUCKETS):
            tile = jnp.where(distance >= LOWS[b], table[:, b : b + 1], tile)
        made.append(jnp.where(distance >= 0, tile, -BIG))
    near, next_one = made
    zero = jnp.zeros((128, 128), F32)
    tile_ref[0:128, 0:128] = zero
    tile_ref[0:128, 128:256] = zero
    tile_ref[128:256, 0:128] = next_one
    tile_ref[128:256, 128:256] = zero
    tile_ref[256:384, 0:128] = near
    tile_ref[256:384, 128:256] = next_one
    tile_ref[384:512, 0:128] = jnp.full((128, 128), -BIG, F32)
    tile_ref[384:512, 128:256] = near


def bucket_sums(near, next_one, far):
    base = lax.broadcasted_iota(jnp.int32, (128, 128), 1) - lax.broadcasted_iota(
        jnp.int32, (128, 128), 0
    )
    lane = lax.broadcasted_iota(jnp.int32, (1, 128), 1)
    out = jnp.zeros((1, 128), F32)
    for b in range(BUCKETS):
        total = jnp.zeros((1, 128), F32)
        for shift, part in ((0, near), (128, next_one)):
            distance = base + shift
            hit = distance >= LOWS[b]
            if b + 1 < BUCKETS:
                hit = hit & (distance < LOWS[b + 1])
            total = total + jnp.sum(jnp.where(hit, part, 0.0), axis=0, keepdims=True)
        if b + 1 == BUCKETS:
            total = total + far
        out = jnp.where(lane == b, jnp.sum(total, axis=1, keepdims=True), out)
    return out


class Rows:
    def __init__(self, ref, first, count):
        self.ref, self.first, self.count = ref, first, count

    def part(self, index):
        devices = 256 // self.count
        block = self.ref[
            pl.ds(index * devices, devices), self.first : self.first + self.count, :
        ]
        return block.reshape(256, 128)


def turn(rows, out_ref):
    for i in range(N * rows.count // 256):
        out_ref[:, i * 256 : i * 256 + 256] = rows.part(i).T


def left_half(rows, out_ref):
    left = left_lanes(256)
    for i in range(N * rows.count // 256):
        out_ref[i * 256 : i * 256 + 256, :] = jnp.where(left, rows.part(i), 0).astype(BF)


def query_out(grad_ref, out_ref, row):
    left = left_lanes(DROW // 2)
    for first in range(0, DEC, 256):
        part = grad_ref[:, first : first + 256].astype(BF)
        rows = jnp.concatenate([part, part], axis=0).T
        for i in range(256 // DROW):
            a = rows[i * DROW : i * DROW + DROW // 2]
            b = rows[i * DROW + DROW // 2 : (i + 1) * DROW]
            out_ref[first // DROW + i, row : row + DROW // 2] = jnp.where(left, a, b)


def finish_rows(high_sum, out_t, grad_t):
    inverse = 1.0 / high_sum
    out_t = out_t * inverse
    scaled = (grad_t.astype(F32) * inverse).astype(BF)
    delta = jnp.sum(scaled.astype(F32) * out_t, axis=0, keepdims=True)
    zero = jnp.zeros_like(scaled)
    rows = jnp.concatenate([zero, scaled], axis=0).T
    return scaled, delta, rows


def self_part(x1, x2, gs, bias_out, t1, t2, mk_s, mq, tiles, scores, e_s, sg, delta_ref, rq, rg, dq):
    turn(x1, t1)
    turn(x2, t2)
    zeros = jnp.zeros((HD, 256), BF)
    left_half(x1, rq)

    for tb in range(DEC // 256):
        span = slice(tb * 256, tb * 256 + 256)
        right = jnp.concatenate([zeros, t1[0:HD, span], mq[:, span]], axis=0)
        high = jnp.full((1, 256), -4.0 * BIG, F32)
        for cu in range(tb + 1):
            rows = slice(cu * 256, cu * 256 + 256)
            s = dot(jnp.concatenate([x1.part(cu), mk_s[rows, :]], axis=1), right)
            if tb - cu < 2:
                at = 256 * (1 - (tb - cu))
                s = s + tiles[at : at + 256, :]
            scores[rows, :] = s
            high = jnp.maximum(high, jnp.max(s, axis=0, keepdims=True))
        total = jnp.zeros((1, 256), F32)
        out_t = jnp.zeros((HD, 256), F32)
        for cu in range(tb + 1):
            rows = slice(cu * 256, cu * 256 + 256)
            e = jnp.exp(scores[rows, :] - high)
            total = total + jnp.sum(e, axis=0, keepdims=True)
            narrow = e.astype(BF)
            e_s[rows, span] = narrow
            out_t = out_t + dot(t2[0:HD, rows], narrow)
        scaled, delta, rows_g = finish_rows(total, out_t, t2[HD:128, span])
        sg[:, span] = scaled
        delta_ref[:, span] = delta
        rg[span, :] = rows_g

    near = jnp.zeros((128, 128), F32)
    next_one = jnp.zeros((128, 128), F32)
    far = jnp.zeros((1, 128), F32)
    dq[...] = jnp.zeros_like(dq)

    def fold(x):
        x = jnp.sum(x, axis=0, keepdims=True)
        return sum(x[:, i : i + 128] for i in range(0, x.shape[1], 128))

    for cu in range(DEC // 256):
        rows = slice(cu * 256, cu * 256 + 256)
        span = slice(cu * 256, DEC)
        width = DEC - cu * 256
        right = jnp.concatenate([sg[:, span], jnp.zeros((HD, width), BF)], axis=0)
        dp = dot(x2.part(cu), right)
        e = e_s[rows, span]
        ds = e.astype(F32) * (dp - delta_ref[:, span])
        narrow = ds.astype(BF)
        part = dot(narrow, rq[span, :]) + dot(e, rg[span, :])
        for i in range(256 // DROW):
            gs[cu * (256 // DROW) + i, 0:DROW] = part[i * DROW : (i + 1) * DROW].astype(BF)
        dq[:, span] += dot(t1[HD:128, rows], narrow)
        near = near + ds[0:128, 0:128] + ds[128:256, 128:256]
        next_one = next_one + ds[0:128, 128:256]
        if width > 256:
            next_one = next_one + ds[128:256, 256:384]
            far = far + fold(ds[0:128, 256:]) + fold(ds[128:256, 384:])
    bias_out[...] = bucket_sums(near, next_one, far)


def cross_rows(x4, t3, t4, mk_c, mq, scores, e_c, sg, delta_ref, rg):
    def block(tb, carry):
        span = pl.ds(pl.multiple_of(tb * 256, 256), 256)
        right = jnp.concatenate([t3[0:HD, span], jnp.zeros((HD, 256), BF), mq[:, span]], axis=0)
        high = jnp.full((1, 256), -4.0 * BIG, F32)
        for cu in range(ENC // 256):
            rows = slice(cu * 256, cu * 256 + 256)
            s = dot(jnp.concatenate([x4.part(cu), mk_c[rows, :]], axis=1), right)
            scores[rows, :] = s
            high = jnp.maximum(high, jnp.max(s, axis=0, keepdims=True))
        total = jnp.zeros((1, 256), F32)
        out_t = jnp.zeros((HD, 256), F32)
        for cu in range(ENC // 256):
            rows = slice(cu * 256, cu * 256 + 256)
            e = jnp.exp(scores[rows, :] - high)
            total = total + jnp.sum(e, axis=0, keepdims=True)
            narrow = e.astype(BF)
            e_c[rows, span] = narrow
            out_t = out_t + dot(t4[HD:128, rows], narrow)
        scaled, delta, rows_g = finish_rows(total, out_t, t3[HD:128, span])
        sg[:, span] = scaled
        delta_ref[:, span] = delta
        rg[span, :] = rows_g
        return carry

    lax.fori_loop(0, DEC // 256, block, 0)


def cross_keys(first, count, xc, t4, g3, e_c, sg, delta_ref, rq, rg, dq):
    size = count * EROW
    rows = pl.ds(pl.multiple_of(first * EROW, EROW), size)
    right = jnp.concatenate([jnp.zeros((HD, DEC), BF), sg[...]], axis=0)
    dp = dot(xc[pl.ds(first, count), 0:EROW, :].reshape(size, 128), right)
    e = e_c[rows, :]
    narrow = (e.astype(F32) * (dp - delta_ref[...])).astype(BF)
    part = dot(narrow, rq[...]) + dot(e, rg[...])
    for i in range(count):
        g3[first + i] = part[i * EROW : (i + 1) * EROW].astype(BF)
    dq[...] += dot(t4[0:HD, rows], narrow)


def fused_kernel(
    q_s, k_s, v_s, g_s, q_c, k_c, v_c, g_c, dec_len, enc_len, rel_bias,
    dqs, dks, dvs, dqc, dkc, dvc, dbias,
    aq, ak, av, ag, bq, bk, bv, bg, dec_v, enc_v, rel_v,
    pc, ps, xc, xs, g3, gs, r3, rs, rb, bias, dp_part, bias_sum,
    t1, t2, t3, t4, mk_s, mk_c, mq, tiles, scores, e_s, e_c, sg, delta_ref, rq, rg, dq,
    in_sem, send_sem, recv_sem, dp_sem, up_sem, down_sem, dp_in,
):
    me, z, c = place()
    my_dp = lax.axis_index("dp")
    greet_near()
    loads = []
    pairs = (
        (k_c, bk), (v_c, bv), (q_c, bq), (g_c, bg), (q_s, aq), (k_s, ak), (v_s, av), (g_s, ag),
        (dec_len, dec_v), (enc_len, enc_v), (rel_bias, rel_v),
    )
    for i, (src, dst) in enumerate(pairs):
        load = pltpu.make_async_copy(src, dst, in_sem.at[i])
        load.start()
        loads.append(load)

    def send_all(which, src, dst, steps):
        copies = []
        for step in steps:
            copy = seq_copy(
                src.at[target_of(*step)], dst.at[me], send_sem, recv_sem, which, step
            )
            copy.start()
            copies.append(copy)
        return copies

    for load in loads[:4]:
        load.wait()
    pack_heads(bk, bv, pc, 0)
    pack_heads(bq, bg, pc, EROW)
    wait_near()
    pass_on(up_sem, down_sem, 2)
    tell(dp_in, dp_peer(1))
    in_c = send_all(0, pc, xc, NEAR)
    for hops in (2, 3, 4):
        heard(up_sem, down_sem, hops)
        if hops < 4:
            pass_on(up_sem, down_sem, hops + 1)
        in_c += send_all(0, pc, xc, at_hops(hops))
    pl.semaphore_wait(dp_in, 1)
    for load in loads[4:]:
        load.wait()
    pack_heads(aq, ak, ps, 0)
    pack_heads(av, ag, ps, DROW)
    xc[me] = pc[me]
    xs[me] = ps[me]
    dec_low, dec_high, dec_low_c, dec_high_c = bounds_of(dec_v)
    enc_low, enc_high, unused_low, unused_high = bounds_of(enc_v)
    key_features(dec_low, dec_high, mk_s, DEC)
    in_s = send_all(1, ps, xs, STEPS)
    key_features(enc_low, enc_high, mk_c, ENC)
    query_features(dec_low_c, dec_high_c, mq)
    bias_tiles(rel_v, me, tiles)
    x1, x2 = Rows(xs, 0, DROW), Rows(xs, DROW, DROW)
    x3, x4 = Rows(xc, EROW, DROW), Rows(xc, 0, EROW)

    left = left_lanes(2 * DROW)
    for dz in (0, 1, 7, 2, 6, 3, 5, 4):
        for copy, step in zip(in_c, IN_ORDER):
            if step[0] == dz:
                copy.wait_recv()
        chip = lax.rem(z + N // 2 - dz, N // 2)
        block = xc[pl.ds(2 * chip, 2), 0:EROW, :].reshape(2 * EROW, 128)
        t4[:, pl.ds(pl.multiple_of(chip * 2 * EROW, 2 * EROW), 2 * EROW)] = block.T
        block = xc[pl.ds(2 * chip, 2), EROW : EROW + DROW, :].reshape(2 * DROW, 128)
        first = pl.multiple_of(chip * 2 * DROW, 2 * DROW)
        t3[:, pl.ds(first, 2 * DROW)] = block.T
        rq[pl.ds(first, 2 * DROW), :] = jnp.where(left, block, 0).astype(BF)
    cross_rows(x4, t3, t4, mk_c, mq, scores, e_c, sg, delta_ref, rg)
    dq[...] = jnp.zeros_like(dq)
    out3, ready = [], []

    for dz in (4, 3, 5, 2, 6, 1, 7, 0):
        chip = lax.rem(z + dz, N // 2)
        for first, count in ((0, 1), (1, 1)) if dz == 4 else ((0, 2),):
            cross_keys(
                2 * chip + first, count, xc, t4, g3, e_c, sg, delta_ref, rq, rg, dq
            )
            out3 += send_all(2, g3, r3, ready)
            if count == 1:
                ready = [(dz, lax.rem(c + first, 2))]
            else:
                ready = [(dz, dc) for dc in (0, 1) if (dz, dc) != (0, 0)]
    query_out(dq, gs, DROW + DROW // 2)
    out3 += send_all(2, g3, r3, ready)
    r3[me] = g3[me]

    for copy in in_s:
        copy.wait_recv()
    self_part(x1, x2, gs, bias, t1, t2, mk_s, mq, tiles, scores, e_s, sg, delta_ref, rq, rg, dq)
    dp_copies = []
    for k in range(1, 4):
        copy = pltpu.make_async_remote_copy(
            src_ref=bias,
            dst_ref=dp_part.at[my_dp],
            send_sem=dp_sem.at[0, k],
            recv_sem=dp_sem.at[1, k],
            device_id=dp_peer(k),
            device_id_type=pl.DeviceIdType.MESH,
        )
        copy.start()
        dp_copies.append(copy)
    dp_part[my_dp] = bias[...]
    query_out(dq, gs, DROW)
    out_s = send_all(3, gs, rs, IN_ORDER[:6])
    rs[me] = gs[me]
    for copy in dp_copies:
        copy.wait()
    total = ((dp_part[0] + dp_part[1]) + dp_part[2]) + dp_part[3]
    bias_sum[...] = total
    rb[me] = total
    out_s += send_all(3, gs, rs, IN_ORDER[6:8])
    out_b = []
    for step in STEPS:
        copy = seq_copy(bias_sum, rb.at[me], send_sem, recv_sem, 4, step)
        copy.start()
        out_b.append(copy)
    out_s += send_all(3, gs, rs, IN_ORDER[8:])
    half = DROW // 2
    for i, dz in enumerate((4, 3, 5, 2, 6, 1, 7, 0)):
        for copy in out3[2 * i : 2 * i + 2]:
            copy.wait_recv()
        chip = lax.rem(z + N // 2 - dz, N // 2)
        unpack_chip(r3, chip, 0, EROW, dkc, 0, dvc, 0)
    for copy in in_c + in_s + out3:
        copy.wait_send()
    for copy in out_b:
        copy.wait()
    rows = jnp.concatenate([rb[i] for i in range(N)], axis=0)
    dbias[...] = rows[:, :BUCKETS] * (1.0 / math.sqrt(4 * DEC))
    for dz in (0, 1, 7, 2, 6, 3, 5, 4):
        for copy, step in zip(out_s, IN_ORDER):
            if step[0] == dz:
                copy.wait_recv()
        chip = lax.rem(z + N // 2 - dz, N // 2)
        unpack_chip(rs, chip, 0, DROW, dks, 0, dvs, 0)
        unpack_chip(rs, chip, DROW, half, dqs, 0, dqs, half)
        unpack_chip(rs, chip, DROW + half, half, dqc, 0, dqc, half)
    for copy in out_s:
        copy.wait_send()


def fused(*arrays):
    vm = pltpu.VMEM
    return pl.pallas_call(
        fused_kernel,
        out_shape=OUT_SHAPES,
        in_specs=[pl.BlockSpec(memory_space=pltpu.HBM)] * 11,
        out_specs=[VM] * 7,
        scratch_shapes=[
            *[vm((DROW, N * HD), BF)] * 5,
            *[vm((EROW, N * HD), BF)] * 2,
            vm((DROW, N * HD), BF),
            vm((1, NEX), jnp.int32),
            vm((1, NEX), jnp.int32),
            vm((N, BUCKETS), F32),
            vm((N, EROW + DROW, 128), BF),
            vm((N, 2 * DROW, 128), BF),
            vm((N, EROW + DROW, 128), BF),
            vm((N, 2 * DROW, 128), BF),
            *[vm((N, EROW, 128), BF)] * 4,
            vm((N, 1, 128), F32),
            vm((1, 128), F32),
            vm((4, 1, 128), F32),
            vm((1, 128), F32),
            *[vm((128, DEC), BF)] * 3,
            vm((128, ENC), BF),
            vm((DEC, 128), BF),
            vm((ENC, 128), BF),
            vm((128, DEC), BF),
            vm((512, 256), F32),
            vm((ENC, 256), F32),
            vm((DEC, DEC), BF),
            vm((ENC, DEC), BF),
            vm((HD, DEC), BF),
            vm((1, DEC), F32),
            vm((DEC, 128), BF),
            vm((DEC, 128), BF),
            vm((HD, DEC), F32),
            pltpu.SemaphoreType.DMA((11,)),
            pltpu.SemaphoreType.DMA((5, N)),
            pltpu.SemaphoreType.DMA((5, N)),
            pltpu.SemaphoreType.DMA((2, 4)),
            pltpu.SemaphoreType.REGULAR((5,)),
            pltpu.SemaphoreType.REGULAR((5,)),
            pltpu.SemaphoreType.REGULAR,
        ],
        compiler_params=pltpu.CompilerParams(collective_id=0, has_side_effects=True, vmem_limit_bytes=32 * 1024 * 1024
        ),
        name="attention_grads",
    )(*arrays)


def on_device(q_s, k_s, v_s, g_s, q_c, k_c, v_c, g_c, dec_len, enc_len, rel_bias):
    flat = [x.reshape(x.shape[1], x.shape[2]) for x in (q_s, k_s, v_s, g_s, q_c, k_c, v_c, g_c)]
    operands = [
        pltpu.with_memory_space_constraint(x, pltpu.HBM)
        for x in (*flat, dec_len, enc_len, rel_bias.T)
    ]
    outs = leave(*fused(*operands))
    return tuple(x.reshape((1,) + x.shape) for x in outs[:6]) + (outs[6].T,)


def solution(mesh):
    rows = P("dp", "seq", "mp")
    return jax.shard_map(
        on_device,
        mesh=mesh,
        in_specs=(rows,) * 8 + (P("dp", None), P("dp", None), P(None, "mp")),
        out_specs=(rows,) * 6 + (P(None, "mp"),),
        check_vma=False,
    )
```
